256 devices in a mesh: lat: 4 (over y), lon: 64 (over z, x, core).
Axes of the slice: x: 4, y: 4, z: 8, core: 2. Of those that a mesh axis runs over, the one named last changes fastest.
Arguments:
- model_state: float32 [5, 4, 3584, 1024], P(None, None, 'lon', 'lat'), may hold values from -6 to 6
- diffusion: float32 [2, 1024], P(None, 'lat'), may hold values from 0.02 to 0.24
- coupling: float32 [4, 5, 5], replicated, may hold values from -2.5 to 2.5
- cutoff: int32 [256], replicated, may hold values from 1 to 896, as said below
- strip_list: int32 [16384, 4], P(('lat', 'lon')), may hold values from 0 to 240, as said below
- nest_place: int32 [256, 64, 2], P(('lat', 'lon')), may hold values from 0 to 1872
Outputs:
- advanced_state: float32 [5, 4, 3584, 1024], P(None, None, 'lon', 'lat')
- nest_boundary: float32 [256, 5, 4, 2048], P(('lat', 'lon'))
The draws below stay inside these ranges and needn't reach their ends.
Inputs may be any that keep to these rules, and one draw needn't show every extreme that they name: cutoff[b] is the number of kept wavenumbers of band row b; the values 1 and 896 both occur. `strip_list`: in the 64 rows of one device: column 0 names an owner (an index of lon) and no owner is named by more than 2 of these rows; at every index of lat some owner is named by exactly 2 rows of every device of that index. Column 1 is a longitude column within the device's block (below 56), column 2 a row offset within the block (at most 240), column 3 a length of 1 to 16; every device has a strip of length 16.
All inputs are finite; a program needn't handle non-finite values.
Results may differ from the reference program's by a relative error of at most 0.0001.
Values sent between devices are 32-bit elements; how exact they have to be, the bound alone decides.
A program may use at most 128 MiB of HBM per device.

```python
import math
import jax
import jax.numpy as jnp
from jax import lax

NLON = 3584
FIELDS = 5
LEVELS = 4
LAT_DEV = 256
POLAR = 128
CAP = 2
STRIP = 16
RATIO = 11
NB = 2048
LON_DEV = 56
NLAT = 1024
KC = 896
SLOTS = 64
N_LAT = 4
N_LON = 64


def draw_cutoff(key, part):
    value_key, place_key = jax.random.split(key)
    strip_values = jax.random.randint(value_key, (2 * POLAR,), 1, KC + 1)
    places = jax.random.permutation(place_key, 2 * POLAR)
    index_line = jnp.arange(2 * POLAR)
    strip_values = jnp.where(index_line == places[0], KC, strip_values)
    strip_values = jnp.where(index_line == places[1], 1, strip_values)
    return strip_values.astype(jnp.int32)


def draw_strip_list(key, part):
    sources = N_LAT * N_LON
    lon_block = NLON // N_LON
    hot_key, source_key, column_key, offset_key, length_key, longest_key = jax.random.split(key, 6)
    hottest = jax.random.randint(hot_key, (N_LAT,), 0, N_LON)
    hot_each = jnp.repeat(hottest, N_LON)

    def one_source(source_seed, hot_owner):
        pick_key, order_key = jax.random.split(source_seed)
        others = (hot_owner + 1 + jnp.arange((N_LON - 1) * CAP) // CAP) % N_LON
        chosen = jax.random.permutation(pick_key, others)[:SLOTS - CAP]
        owners = jnp.concatenate([jnp.zeros((CAP,), jnp.int32) + hot_owner, chosen.astype(jnp.int32)])
        return jax.random.permutation(order_key, owners)
    owners = jax.vmap(one_source)(jax.random.split(source_key, sources), hot_each)
    columns = jax.random.randint(column_key, (sources, SLOTS), 0, lon_block)
    offsets = jax.random.randint(offset_key, (sources, SLOTS), 0, LAT_DEV - STRIP + 1)
    lengths = jax.random.randint(length_key, (sources, SLOTS), 1, STRIP + 1)
    longest = jax.random.randint(longest_key, (sources, 1), 0, SLOTS)
    lengths = jnp.where(jnp.arange(SLOTS)[None, :] == longest, STRIP, lengths)
    stacked = jnp.stack([owners.astype(jnp.int32), columns.astype(jnp.int32), offsets.astype(jnp.int32), lengths.astype(jnp.int32)], axis=-1)
    return stacked.reshape(sources * SLOTS, 4).astype(jnp.int32)


def set_ends(result, own_key, low, high):
    index_at = [jax.random.randint(jax.random.fold_in(own_key, axis), (), 0, length) for axis, length in enumerate(result.shape)]
    main_axis = result.shape.index(max(result.shape))
    next_to = index_at[:main_axis] + [(index_at[main_axis] + 1) % result.shape[main_axis]] + index_at[main_axis + 1:]
    return result.at[tuple(index_at)].set(low).at[tuple(next_to)].set(high)


def shard_levels(own_key, shape, cuts, least, high):
    def one(dim, blocks):
        heights = jax.random.uniform(jax.random.fold_in(jax.random.fold_in(own_key, 6), dim), (blocks,), jnp.float32, least / len(cuts), high / len(cuts))
        return jnp.repeat(jnp.exp(heights), shape[dim] // blocks).reshape((-1,) + (1,) * (len(shape) - dim - 1))

    level = one(*cuts[0])
    for cut in cuts[1:]:
        level = level * one(*cut)
    return level


def centred(rng, shape, width, bound, pieces=(), kind=jnp.bfloat16):
    gain = shard_levels(rng, shape, pieces, -0.22, 0.18) if pieces else 1.0
    array = jax.random.normal(rng, shape, jnp.float32) * width * gain
    return jnp.minimum(jnp.maximum(array, -bound), bound).astype(kind)


def setup_inputs(seed: int = 0) -> dict:
    splits = jax.random.split(jax.random.key(seed), 7)
    return {
        "model_state": centred(splits[0], (FIELDS, LEVELS, NLON, NLAT), 1.0, 6.0, ((2, 64), (3, 4)), jnp.float32),
        "diffusion": jnp.clip(jnp.exp(math.log(0.24) - 2.4849066 * jax.random.uniform(splits[1], (2, NLAT), jnp.float32) ** shard_levels(splits[1], (2, NLAT), ((1, 4),), -0.2, 0.2)), 0.02, 0.24),
        "coupling": centred(splits[2], (LEVELS, FIELDS, FIELDS), FIELDS ** -0.5, 2.5, (), jnp.float32),
        "cutoff": draw_cutoff(jax.random.fold_in(splits[6], 71), 0),
        "strip_list": draw_strip_list(jax.random.fold_in(splits[6], 71), 0),
        "nest_place": set_ends(jax.random.randint(splits[5], (N_LAT * N_LON, N_LON, CAP), 0, NB - STRIP * RATIO + 1), jax.random.fold_in(splits[5], 1), 0, NB - STRIP * RATIO).astype(jnp.int32),
    }


def nest_forcing(updated, strip_list, nest_place):
    top_wavenumber_kept = lax.Precision.HIGHEST
    lists = strip_list.reshape(N_LAT, N_LON, SLOTS, 4)
    lat_ids = jnp.arange(N_LAT, dtype=jnp.int32)[:, None, None]
    lon_ids = jnp.arange(N_LON, dtype=jnp.int32)[None, :, None]
    owners = lists[..., 0]
    columns = (lon_ids * LON_DEV + lists[..., 1]).astype(jnp.int32)
    offsets = (lat_ids * LAT_DEV + lists[..., 2]).astype(jnp.int32)
    lengths = lists[..., 3]
    zero = jnp.zeros((), jnp.int32)

    def cut_strip(column, offset):
        return lax.dynamic_slice(updated, (zero, zero, column, offset), (FIELDS, LEVELS, 1, STRIP))[:, :, 0, :]

    boundary_strips = jax.vmap(cut_strip)(columns.reshape(-1), offsets.reshape(-1))
    positions = jnp.arange(STRIP, dtype=jnp.int32)
    boundary_strips = jnp.where(positions[None, None, None, :] < lengths.reshape(-1)[:, None, None, None], boundary_strips, 0.0)
    slot_ids = jnp.arange(SLOTS, dtype=jnp.int32)
    earlier = slot_ids[None, :] < slot_ids[:, None]
    same = owners[..., :, None] == owners[..., None, :]
    rank = jnp.sum((same & earlier).astype(jnp.int32), axis=-1)
    owner_rows = (lat_ids * N_LON + owners).astype(jnp.int32)
    begins = nest_place[owner_rows, jnp.broadcast_to(lon_ids, owners.shape), rank]
    nest_points = jnp.arange(STRIP * RATIO, dtype=jnp.int32)
    filter_table = jnp.maximum(RATIO - jnp.abs(nest_points[None, :] - positions[:, None] * RATIO), 0).astype(jnp.float32) / RATIO
    sources = N_LAT * N_LON
    boundary_strips = boundary_strips.reshape(sources, SLOTS, FIELDS, LEVELS, STRIP)
    owner_rows = owner_rows.reshape(sources, SLOTS)
    begins = begins.reshape(sources, SLOTS)

    def add_source(strip_index, total):
        strip_values = jnp.einsum("icvj,jk->ikcv", boundary_strips[strip_index], filter_table, precision=top_wavenumber_kept)
        return total.at[owner_rows[strip_index][:, None], begins[strip_index][:, None] + nest_points[None, :]].add(strip_values)

    total = lax.fori_loop(0, sources, add_source, jnp.zeros((sources, NB, FIELDS, LEVELS), jnp.float32))
    return jnp.transpose(total, (0, 2, 3, 1))


def reference(model_state, diffusion, coupling, cutoff, strip_list, nest_place):
    top_wavenumber_kept = lax.Precision.HIGHEST
    east = jnp.roll(model_state, -1, axis=2)
    west = jnp.roll(model_state, 1, axis=2)
    padded = jnp.pad(model_state, ((0, 0), (0, 0), (0, 0), (1, 1)))
    blended = jnp.einsum("lfg,glij->flij", coupling, model_state, precision=top_wavenumber_kept)
    updated = model_state + diffusion[0] * (east + west - 2.0 * model_state) + diffusion[1] * (padded[..., :-2] + padded[..., 2:] - 2.0 * model_state) + blended
    rows = jnp.concatenate([updated[..., :POLAR], updated[..., NLAT - POLAR:]], axis=3)
    spectrum = jnp.fft.rfft(rows, axis=2)
    wavenumber = jnp.arange(NLON // 2 + 1, dtype=jnp.int32)[:, None]
    spectrum = jnp.where(wavenumber < cutoff[None, :], spectrum, 0.0)
    filtered = jnp.fft.irfft(spectrum, n=NLON, axis=2).astype(updated.dtype)
    advanced_state = updated.at[..., :POLAR].set(filtered[..., :POLAR])
    advanced_state = advanced_state.at[..., NLAT - POLAR:].set(filtered[..., POLAR:])
    boundary = nest_forcing(updated, strip_list, nest_place)
    return advanced_state, boundary
```

```python
import jax
import jax.numpy as jnp
import ml_dtypes
import numpy as np
from jax import lax
from jax.experimental import pallas as pl
from jax.experimental.pallas import tpu as pltpu
from jax.sharding import PartitionSpec as P

MESH = pl.DeviceIdType.MESH
F32, BF16 = jnp.float32, jnp.bfloat16
FIELDS, LEVELS, COLS, ROWS = 5, 4, 56, 256
NLON, NDEV, POLAR, NB, RATIO, STRIP = 3584, 64, 128, 2048, 11, 16
PAIRS = FIELDS * LEVELS // 2
QROWS = 40
K1 = 28
CHUNKS = 4


def hi_lo(table):
    hi = table.astype(np.float32).astype(ml_dtypes.bfloat16)
    lo = (table - hi.astype(np.float64)).astype(np.float32).astype(ml_dtypes.bfloat16)
    return hi, lo


def tables():
    q = np.arange(QROWS)
    live = (q <= 32).astype(np.float64)
    c = np.arange(NDEV)
    lane = np.arange(128)
    unit, mu = lane // 64, lane % 64
    m = np.where(mu == 57, -1, mu)
    live_in = (mu <= 57).astype(np.float64)
    live_out = (mu < COLS).astype(np.float64)
    turn = 2 * np.pi * np.outer(q, c) / NDEV
    c1 = np.concatenate([np.cos(turn) * live[:, None], -np.sin(turn) * live[:, None]], 0)
    weight = np.where((q == 0) | (q == 32), 1.0, 2.0) * live / NLON
    c2 = np.concatenate([np.cos(turn) * weight[:, None], -np.sin(turn) * weight[:, None]], 0).T
    phi = 2 * np.pi * np.outer(q, m) / NLON
    twiddle = np.stack([np.cos(phi), np.sin(phi)]) * live[None, :, None]
    out = np.arange(128)
    unit_k, part_k, j = out // 64, (out % 64) // 32, out % 32
    k1 = j - 14
    live_k = (j < K1).astype(np.float64)
    psi = 2 * np.pi * np.outer(m, k1) / COLS
    same = (unit[:, None] == unit_k[None, :]) * live_k[None, :]
    cos, sin = np.cos(psi) * same, np.sin(psi) * same
    real = part_k[None, :] == 0
    b1 = np.concatenate([np.where(real, cos, -sin), np.where(real, sin, cos)], 0)
    b1 = b1 * np.tile(live_in, 2)[:, None]
    b2 = np.concatenate([np.where(real, cos, -sin).T, np.where(real, sin, cos).T], 1)
    b2 = b2 * np.tile(live_out, 2)[None, :]
    wave = np.abs(q[:, None] + 64 * k1[None, :])
    wave = np.where((live[:, None] > 0) & (live_k[None, :] > 0), wave, 1 << 20).astype(np.int32)

    def left(t):
        hi, lo = hi_lo(t)
        return np.concatenate([hi, hi, lo], 1)

    def right(t):
        hi, lo = hi_lo(t)
        return np.concatenate([hi, hi, lo], 0)

    return left(c1), twiddle.astype(np.float32), right(b1), wave, right(b2), left(c2)


def split(x):
    hi = x.astype(BF16)
    return hi, (x - hi.astype(F32)).astype(BF16)


def iota(shape, dim):
    return lax.broadcasted_iota(jnp.int32, shape, dim)


def dot(a, b):
    return jnp.dot(a, b, preferred_element_type=F32)


def place_of(device):
    return lax.rem(device, CHUNKS) * (NDEV // CHUNKS) + lax.div(device, CHUNKS)


def step_kernel(
    ms, dif, coup, cut, sl, npl, c1, tw, b1, wave, b2, c2,
    out, nest,
    pk, rl, arr, res, ret, zb, sn, ss, hw, he, hn, hs, xs, sb, rb, tb, lb,
    s_rel, r_rel, s_fwd, r_fwd, s_ret, r_ret, s_nest, r_nest, s_halo, r_halo,
):
    la, me = lax.axis_index("lat"), lax.axis_index("lon")
    polar_lat = jnp.where(la < 2, 0, 3)
    helper_lat = jnp.where(la < 2, 1, 2)
    is_polar = la == polar_lat
    is_helper = jnp.logical_not(is_polar)
    half = jnp.where(is_polar, 0, 1)
    start = pl.multiple_of(jnp.where(la == 3, ROWS - POLAR, 0), 128)
    has_north, has_south = la > 0, la < 3
    mine = place_of(me)

    def remote(src, dst, s, r, lat, lon):
        return pltpu.make_async_remote_copy(
            src, dst, s, r, device_id={"lat": lat, "lon": lon}, device_id_type=MESH
        )

    barrier = pltpu.get_barrier_semaphore()

    def greet(lat, lon):
        pl.semaphore_signal(barrier, device_id={"lat": lat, "lon": lon}, device_id_type=MESH)

    @pl.when(has_north)
    def _():
        greet(la - 1, me)

    @pl.when(has_south)
    def _():
        greet(la + 1, me)

    def greet_plane(k, carry):
        greet(la, lax.rem(me + k, NDEV))
        return carry

    lax.fori_loop(1, NDEV, greet_plane, 0)

    d0, d1 = dif[0:1, :], dif[1:2, :]
    lane_row = iota((COLS, ROWS), 1)
    col = iota((COLS, ROWS), 0)
    lane_u = iota((COLS, 128), 1)
    sn[...] = jnp.zeros_like(sn)
    ss[...] = jnp.zeros_like(ss)

    def level(l, carry):
        x = [ms[g, l] for g in range(FIELDS)]
        for f in range(FIELDS):
            own = x[f]
            east = jnp.where(col == COLS - 1, 0.0, pltpu.roll(own, COLS - 1, 0))
            west = jnp.where(col == 0, 0.0, pltpu.roll(own, 1, 0))
            south = jnp.where(lane_row == ROWS - 1, 0.0, pltpu.roll(own, ROWS - 1, 1))
            north = jnp.where(lane_row == 0, 0.0, pltpu.roll(own, 1, 1))
            acc = own + d0 * (east + west - 2.0 * own) + d1 * (north + south - 2.0 * own)
            for g in range(FIELDS):
                acc = acc + coup[l, f, g] * x[g]
            out[f, l] = acc
            u = f * LEVELS + l
            sn[...] = jnp.where(lane_u == u, own[:, 0:1], sn[...])
            ss[...] = jnp.where(lane_u == u, own[:, ROWS - 1 : ROWS], ss[...])
        return carry

    lax.fori_loop(0, LEVELS, level, 0)

    @pl.when(is_polar)
    def _():
        tail_row = iota((8, 128), 0)
        d0p = dif[0:1, pl.ds(start, POLAR)]

        def pack(k, carry):
            f, l0 = lax.div(k, 2), 2 * lax.rem(k, 2)
            rows = []
            for p in range(2):
                first = ms[f, l0 + p, 0:1, pl.ds(start, POLAR)]
                last = ms[f, l0 + p, COLS - 1 : COLS, pl.ds(start, POLAR)]
                tail = jnp.where(tail_row == 0, last, jnp.where(tail_row == 1, first, 0.0)) * d0p
                rows += [out[f, l0 + p, :, pl.ds(start, POLAR)], tail]
            turned = jnp.concatenate(rows, 0).T
            pk[k, 0] = turned[:NDEV]
            pk[k, 1] = turned[NDEV:]
            return carry

        lax.fori_loop(0, PAIRS, pack, 0)

    pl.semaphore_wait(barrier, NDEV - 1 + jnp.where(is_polar, 1, 2))

    east_dev, west_dev = lax.rem(me + 1, NDEV), lax.rem(me + NDEV - 1, NDEV)
    to_east = remote(ms.at[:, :, pl.ds(COLS - 1, 1)], hw, s_halo.at[0], r_halo.at[0], la, east_dev)
    to_west = remote(ms.at[:, :, pl.ds(0, 1)], he, s_halo.at[1], r_halo.at[1], la, west_dev)
    to_south = remote(ss, hn, s_halo.at[2], r_halo.at[2], jnp.minimum(la + 1, 3), me)
    to_north = remote(sn, hs, s_halo.at[3], r_halo.at[3], jnp.maximum(la - 1, 0), me)

    size = NDEV // CHUNKS

    def relay(g):
        rows = pl.ds(g * size, size)
        return remote(pk.at[:, 1, rows], rl.at[:, rows], s_rel.at[g], r_rel.at[g], helper_lat, me)

    @pl.when(is_polar)
    def _():
        for g in range(CHUNKS):
            relay(g).start()

    to_east.start()
    to_west.start()
    pl.when(has_south)(to_south.start)
    pl.when(has_north)(to_north.start)

    @pl.when(is_polar)
    def _():
        pltpu.make_async_copy(pk.at[:, 0, mine], arr.at[:, me], r_fwd).start()

        def send(k, carry):
            d = lax.rem(me + k, NDEV)
            remote(pk.at[:, 0, place_of(d)], arr.at[:, me], s_fwd, r_fwd, la, d).start()
            return carry

        lax.fori_loop(1, NDEV, send, 0)

    @pl.when(is_helper)
    def _():
        for g in range(CHUNKS):
            relay(g).wait_recv()

            def send(i, carry, g=g):
                b = lax.rem(i + lax.div(me, CHUNKS), size)
                d = b * CHUNKS + g

                @pl.when(d != me)
                def _():
                    remote(rl.at[:, g * size + b], arr.at[:, me], s_fwd, r_fwd, la, d).start()

                return carry

            lax.fori_loop(0, size, send, 0)
        pltpu.make_async_copy(rl.at[:, mine], arr.at[:, me], r_fwd).start()

    to_east.wait_recv()
    to_west.wait_recv()
    for f in range(FIELDS):
        for l in range(LEVELS):
            out[f, l, 0:1] += d0 * hw[f, l]
            out[f, l, COLS - 1 : COLS] += d0 * he[f, l]

    @pl.when(has_north)
    def _():
        to_south.wait_recv()
        halo = hn[...]
        d = dif[1:2, 0:128]

        def fix(u, carry):
            f, l = lax.div(u, LEVELS), lax.rem(u, LEVELS)
            value = pltpu.roll(halo, lax.rem(128 - u, 128), 1)
            out[f, l, :, 0:128] += jnp.where(lane_u == 0, d * value, 0.0)
            return carry

        lax.fori_loop(0, FIELDS * LEVELS, fix, 0)

    @pl.when(has_south)
    def _():
        to_north.wait_recv()
        halo = hs[...]
        d = dif[1:2, 128:256]

        def fix(u, carry):
            f, l = lax.div(u, LEVELS), lax.rem(u, LEVELS)
            value = pltpu.roll(halo, 127 - u, 1)
            out[f, l, :, 128:256] += jnp.where(lane_u == 127, d * value, 0.0)
            return carry

        lax.fori_loop(0, FIELDS * LEVELS, fix, 0)

    owners = sl[:, 0:1].astype(F32)
    columns, offsets, lengths = sl[:, 1:2], sl[:, 2:3], sl[:, 3:4]
    eye = iota((NDEV, NDEV), 0) == iota((NDEV, NDEV), 1)
    owner_row = jnp.sum(jnp.where(eye, owners, 0.0), axis=0, keepdims=True)
    before = (owners == owner_row) & (iota((NDEV, NDEV), 1) < iota((NDEV, NDEV), 0))
    rank = jnp.sum(jnp.where(before, 1.0, 0.0), axis=1, keepdims=True)
    slot = rank * NDEV + owners
    twice = iota((NDEV, 128), 0) == lax.rem(iota((NDEV, 128), 1), NDEV)
    slot_row = jnp.sum(jnp.where(twice, slot, 0.0), axis=0, keepdims=True)
    routing = jnp.where(iota((128, 128), 0).astype(F32) == slot_row, 1.0, 0.0).astype(BF16)
    pick = jnp.where(lax.rem(iota((NDEV, 128), 1), NDEV) == columns, 1.0, 0.0).astype(BF16)
    high = offsets >= 128
    inner = lax.rem(offsets, 128)
    lane = iota((NDEV, 128), 1)
    spill = (lane < STRIP) & (inner > 128 - STRIP)
    bits = lax.div(inner, 1)
    zero8 = jnp.zeros((8, ROWS), F32)

    def strips_of(u, carry):
        x = out[lax.div(u, LEVELS), lax.rem(u, LEVELS)]
        top = x.astype(BF16).astype(F32)
        y = dot(pick, jnp.concatenate([top, zero8, x - top, zero8], 0).astype(BF16))
        a = jnp.where(high, y[:, 128:], y[:, :128])
        a = jnp.where(spill, y[:, 128:], a)
        for shift in (64, 32, 16):
            a = jnp.where((bits & shift) != 0, pltpu.roll(a, 128 - shift, 1), a)
        xs[u] = a
        return carry

    lax.fori_loop(0, FIELDS * LEVELS, strips_of, 0)
    window = lax.div(lane, 32)
    for g in range(3):
        both = []
        for h in range(2):
            a = jnp.zeros((NDEV, 128), F32)
            for i in range(4):
                u = 8 * g + 2 * i + h
                if u < FIELDS * LEVELS:
                    v = xs[u] if i == 0 else pltpu.roll(xs[u], 32 * i, 1)
                    a = jnp.where(window == i, v, a)
            for shift in (8, 4, 2, 1):
                a = jnp.where((bits & shift) != 0, pltpu.roll(a, 128 - shift, 1), a)
            both.append(a)
        a = jnp.where(lax.rem(lane, 32) < 16, both[0], pltpu.roll(both[1], 16, 1))
        a = jnp.where(lax.rem(lane, STRIP) < lengths, a, 0.0)
        a = dot(routing, jnp.concatenate(split(a), 0))
        sb[g, 0] = a[:NDEV]
        sb[g, 1] = a[NDEV:]

    pltpu.make_async_copy(sb.at[:, :, me], rb.at[:, :, me], r_nest).start()

    def send_strips(k, carry):
        d = lax.rem(me + k, NDEV)
        remote(sb.at[:, :, d], rb.at[:, :, me], s_nest, r_nest, la, d).start()
        return carry

    lax.fori_loop(1, NDEV, send_strips, 0)

    pltpu.make_async_copy(arr, arr, r_fwd).wait()
    cos, sin = tw[0], tw[1]

    def forward(k, carry):
        hi, lo = split(arr[k])
        y = dot(c1[...], jnp.concatenate([hi, lo, hi], 0))
        re, im = y[:QROWS], y[QROWS:]
        zb[k, :, 0:128] = re * cos + im * sin
        zb[k, :, 128:256] = im * cos - re * sin
        return carry

    lax.fori_loop(0, PAIRS, forward, 0)
    hi, lo = split(zb[...].reshape(PAIRS * QROWS, 256))
    spectrum = dot(jnp.concatenate([hi, lo, hi], 1), b1[...])
    base = jnp.where(la < 2, 0, POLAR) + half * NDEV
    keep = wave[...] < cut[base + mine]
    spectrum = jnp.where(keep[None], spectrum.reshape(PAIRS, QROWS, 128), 0.0)
    hi, lo = split(spectrum.reshape(PAIRS * QROWS, 128))
    zb[...] = dot(jnp.concatenate([hi, lo, hi], 1), b2[...]).reshape(PAIRS, QROWS, 256)

    def backward(k, carry):
        re, im = zb[k, :, 0:128], zb[k, :, 128:256]
        turned = jnp.concatenate([re * cos - im * sin, re * sin + im * cos], 0)
        hi, lo = split(turned)
        res[k] = dot(c2[...], jnp.concatenate([hi, lo, hi], 0))
        return carry

    lax.fori_loop(0, PAIRS, backward, 0)

    @pl.when(is_polar)
    def _():
        pltpu.make_async_copy(res.at[:, me], ret.at[:, 0, mine], r_ret).start()

    @pl.when(is_helper)
    def _():
        remote(res.at[:, me], ret.at[:, 1, mine], s_ret, r_ret, polar_lat, me).start()

    def send_back(k, carry):
        d = lax.rem(me + k, NDEV)
        remote(res.at[:, d], ret.at[:, half, mine], s_ret, r_ret, polar_lat, d).start()
        return carry

    lax.fori_loop(1, NDEV, send_back, 0)

    pltpu.make_async_copy(rb, rb, r_nest).wait()
    for g in range(3):
        tb[g] = jnp.concatenate([rb[g, 0], rb[g, 1]], 0).T
    for t in range(STRIP):
        x = jnp.concatenate([tb[g, pl.ds(t, 8, stride=STRIP), :] for g in range(3)], 0)
        top = x.astype(BF16).astype(F32)
        lb[:, t * 128 : (t + 1) * 128] = jnp.concatenate([top, x - top], 0).astype(BF16)
    places = npl[0].astype(F32)
    lane_c = iota((NDEV, 128), 1)
    chosen = jnp.where(lane_c < NDEV, places[:, 0:1], places[:, 1:2])
    begin = jnp.sum(jnp.where(twice, chosen, 0.0), axis=0, keepdims=True)
    wide = 256
    point = iota((wide, 128), 0).astype(F32)

    def boundary(n, carry):
        first = pl.multiple_of(n * wide, wide)
        away = point + (n * wide).astype(F32) - begin
        hats = []
        for t in range(STRIP):
            d = away - float(RATIO * t)
            hat = jnp.maximum(float(RATIO) - jnp.abs(d), 0.0)
            if t == 0:
                hat = jnp.where(d >= 0.0, hat, 0.0)
            hats.append(hat.astype(BF16))
        total = lax.dot_general(
            lb[...], jnp.concatenate(hats, 1), (((1,), (1,)), ((), ())), preferred_element_type=F32
        )
        total = (total[:24] + total[24:]) * (1.0 / RATIO)
        for f in range(FIELDS):
            nest[0, f, :, pl.ds(first, wide)] = total[f * LEVELS : (f + 1) * LEVELS]
        return carry

    lax.fori_loop(0, NB // wide, boundary, 0)

    @pl.when(is_polar)
    def _():
        pltpu.make_async_copy(ret, ret, r_ret).wait()

        def unpack(k, carry):
            f, l0 = lax.div(k, 2), 2 * lax.rem(k, 2)
            turned = jnp.concatenate([ret[k, 0], ret[k, 1]], 0).T
            out[f, l0, :, pl.ds(start, POLAR)] = turned[:COLS]
            out[f, l0 + 1, :, pl.ds(start, POLAR)] = turned[64 : 64 + COLS]
            return carry

        lax.fori_loop(0, PAIRS, unpack, 0)

    to_east.wait_send()
    to_west.wait_send()
    pl.when(has_south)(to_south.wait_send)
    pl.when(has_north)(to_north.wait_send)
    others = pl.ds(0, NDEV - 1)
    pltpu.make_async_copy(res.at[:, others], res.at[:, others], s_fwd).wait()
    pltpu.make_async_copy(sb.at[:, :, others], sb.at[:, :, others], s_nest).wait()

    @pl.when(is_polar)
    def _():
        for g in range(CHUNKS):
            relay(g).wait_send()
        pltpu.make_async_copy(res.at[:, others], res.at[:, others], s_ret).wait()

    @pl.when(is_helper)
    def _():
        pltpu.make_async_copy(res, res, s_ret).wait()


def local(model_state, diffusion, coupling, cutoff, strip_list, nest_place):
    vmem = pl.BlockSpec(memory_space=pltpu.VMEM)
    smem = pl.BlockSpec(memory_space=pltpu.SMEM)
    dma = pltpu.SemaphoreType.DMA
    constants = [jnp.asarray(t) for t in tables()]
    return pl.pallas_call(
        step_kernel,
        name="dynamics_step",
        out_shape=[
            jax.ShapeDtypeStruct(model_state.shape, F32),
            jax.ShapeDtypeStruct((1, FIELDS, LEVELS, NB), F32),
        ],
        in_specs=[vmem, vmem, smem, smem, vmem, vmem] + [vmem] * len(constants),
        out_specs=[vmem, vmem],
        scratch_shapes=[
            pltpu.VMEM((PAIRS, 2, NDEV, 128), F32),
            pltpu.VMEM((PAIRS, NDEV, 128), F32),
            pltpu.VMEM((PAIRS, NDEV, 128), F32),
            pltpu.VMEM((PAIRS, NDEV, 128), F32),
            pltpu.VMEM((PAIRS, 2, NDEV, 128), F32),
            pltpu.VMEM((PAIRS, QROWS, 256), F32),
            pltpu.VMEM((COLS, 128), F32),
            pltpu.VMEM((COLS, 128), F32),
            pltpu.VMEM((FIELDS, LEVELS, 1, ROWS), F32),
            pltpu.VMEM((FIELDS, LEVELS, 1, ROWS), F32),
            pltpu.VMEM((COLS, 128), F32),
            pltpu.VMEM((COLS, 128), F32),
            pltpu.VMEM((FIELDS * LEVELS, NDEV, 128), F32),
            pltpu.VMEM((3, 2, NDEV, 128), F32),
            pltpu.VMEM((3, 2, NDEV, 128), F32),
            pltpu.VMEM((3, 128, 128), F32),
            pltpu.VMEM((48, STRIP * 128), BF16),
            dma((CHUNKS,)), dma((CHUNKS,)),
            dma, dma, dma, dma, dma, dma,
            dma((4,)), dma((4,)),
        ],
        compiler_params=pltpu.CompilerParams(
            collective_id=0, has_side_effects=True, vmem_limit_bytes=48 << 20
        ),
    )(model_state, diffusion, coupling, cutoff, strip_list, nest_place, *constants)


def solution(mesh):
    return jax.shard_map(
        local,
        mesh=mesh,
        in_specs=(
            P(None, None, "lon", "lat"),
            P(None, "lat"),
            P(),
            P(),
            P(("lat", "lon"), None),
            P(("lat", "lon"), None, None),
        ),
        out_specs=(P(None, None, "lon", "lat"), P(("lat", "lon"), None, None, None)),
        check_vma=False,
    )
```

```python
import jax
import jax.numpy as jnp
import ml_dtypes
import numpy as np
from jax import lax
from jax.experimental import pallas as pl
from jax.experimental.pallas import tpu as pltpu
from jax.sharding import PartitionSpec as P

MESH = pl.DeviceIdType.MESH
F32, BF16 = jnp.float32, jnp.bfloat16
FIELDS, LEVELS, COLS, ROWS = 5, 4, 56, 256
NLON, NDEV, POLAR, NB, RATIO, STRIP = 3584, 64, 128, 2048, 11, 16
PAIRS = FIELDS * LEVELS // 2
QROWS = 40
K1 = 28
CHUNKS = 4


def hi_lo(table):
    hi = table.astype(np.float32).astype(ml_dtypes.bfloat16)
    lo = (table - hi.astype(np.float64)).astype(np.float32).astype(ml_dtypes.bfloat16)
    return hi, lo


def tables():
    q = np.arange(QROWS)
    live = (q <= 32).astype(np.float64)
    c = np.arange(NDEV)
    lane = np.arange(128)
    unit, mu = lane // 64, lane % 64
    m = np.where(mu == 57, -1, mu)
    live_in = (mu <= 57).astype(np.float64)
    live_out = (mu < COLS).astype(np.float64)
    turn = 2 * np.pi * np.outer(q, c) / NDEV
    c1 = np.concatenate([np.cos(turn) * live[:, None], -np.sin(turn) * live[:, None]], 0)
    weight = np.where((q == 0) | (q == 32), 1.0, 2.0) * live / NLON
    c2 = np.concatenate([np.cos(turn) * weight[:, None], -np.sin(turn) * weight[:, None]], 0).T
    phi = 2 * np.pi * np.outer(q, m) / NLON
    twiddle = np.stack([np.cos(phi), np.sin(phi)]) * live[None, :, None]
    out = np.arange(128)
    unit_k, part_k, j = out // 64, (out % 64) // 32, out % 32
    k1 = j - 14
    live_k = (j < K1).astype(np.float64)
    psi = 2 * np.pi * np.outer(m, k1) / COLS
    same = (unit[:, None] == unit_k[None, :]) * live_k[None, :]
    cos, sin = np.cos(psi) * same, np.sin(psi) * same
    real = part_k[None, :] == 0
    b1 = np.concatenate([np.where(real, cos, -sin), np.where(real, sin, cos)], 0)
    b1 = b1 * np.tile(live_in, 2)[:, None]
    b2 = np.concatenate([np.where(real, cos, -sin).T, np.where(real, sin, cos).T], 1)
    b2 = b2 * np.tile(live_out, 2)[None, :]
    def left(t):
        hi, lo = hi_lo(t)
        return np.concatenate([hi, hi, lo], 1)

    def right(t):
        hi, lo = hi_lo(t)
        return np.concatenate([hi, hi, lo], 0)

    return left(c1), twiddle.astype(np.float32), right(b1), right(b2), left(c2)


def split(x):
    hi = x.astype(BF16)
    return hi, (x - hi.astype(F32)).astype(BF16)


def iota(shape, dim):
    return lax.broadcasted_iota(jnp.int32, shape, dim)


def dot(a, b):
    return jnp.dot(a, b, preferred_element_type=F32)


def place_of(device):
    return lax.rem(device, CHUNKS) * (NDEV // CHUNKS) + lax.div(device, CHUNKS)


def step_kernel(
    ms_hbm, dif_hbm, coup_hbm, cut_hbm, sl_hbm, npl_hbm, c1_hbm, tw_hbm, b1_hbm, b2_hbm, c2_hbm,
    out, nest,
    ms, dif, coup, cut, sl, npl, c1, tw, b1, b2, c2, s_load,
    pk, rl, arr, res, ret, zb, sn, ss, hw, he, hn, hs, xs, sb, rb, tb, lb,
    s_rel, r_rel, s_fwd, r_fwd, s_ret, r_ret, s_nest, r_nest, s_halo, r_halo,
):
    la, me = lax.axis_index("lat"), lax.axis_index("lon")
    polar_lat = jnp.where(la < 2, 0, 3)
    helper_lat = jnp.where(la < 2, 1, 2)
    is_polar = la == polar_lat
    is_helper = jnp.logical_not(is_polar)
    half = jnp.where(is_polar, 0, 1)
    start = pl.multiple_of(jnp.where(la == 3, ROWS - POLAR, 0), 128)
    has_north, has_south = la > 0, la < 3
    mine = place_of(me)

    def remote(src, dst, s, r, lat, lon):
        return pltpu.make_async_remote_copy(
            src, dst, s, r, device_id={"lat": lat, "lon": lon}, device_id_type=MESH
        )

    early = [(ms_hbm, ms), (dif_hbm, dif), (coup_hbm, coup)]
    late = [(cut_hbm, cut), (sl_hbm, sl), (npl_hbm, npl), (c1_hbm, c1), (tw_hbm, tw)]
    late += [(b1_hbm, b1), (b2_hbm, b2), (c2_hbm, c2)]
    loads = [pltpu.make_async_copy(a, b, s_load.at[i]) for i, (a, b) in enumerate(early + late)]
    for load in loads:
        load.start()

    barrier = pltpu.get_barrier_semaphore()

    def greet(lat, lon):
        pl.semaphore_signal(barrier, device_id={"lat": lat, "lon": lon}, device_id_type=MESH)

    @pl.when(has_north)
    def _():
        greet(la - 1, me)

    @pl.when(has_south)
    def _():
        greet(la + 1, me)

    def greet_plane(k, carry):
        greet(la, lax.rem(me + k, NDEV))
        return carry

    lax.fori_loop(1, NDEV, greet_plane, 0)
    for load in loads[: len(early)]:
        load.wait()

    d0, d1 = dif[0:1, :], dif[1:2, :]
    lane_row = iota((COLS, ROWS), 1)
    col = iota((COLS, ROWS), 0)
    lane_u = iota((COLS, 128), 1)
    sn[...] = jnp.zeros_like(sn)
    ss[...] = jnp.zeros_like(ss)

    def level(l, carry):
        x = [ms[g, l] for g in range(FIELDS)]
        for f in range(FIELDS):
            own = x[f]
            east = jnp.where(col == COLS - 1, 0.0, pltpu.roll(own, COLS - 1, 0))
            west = jnp.where(col == 0, 0.0, pltpu.roll(own, 1, 0))
            south = jnp.where(lane_row == ROWS - 1, 0.0, pltpu.roll(own, ROWS - 1, 1))
            north = jnp.where(lane_row == 0, 0.0, pltpu.roll(own, 1, 1))
            acc = own + d0 * (east + west - 2.0 * own) + d1 * (north + south - 2.0 * own)
            for g in range(FIELDS):
                acc = acc + coup[f, l, g] * x[g]
            out[f, l] = acc
            u = f * LEVELS + l
            sn[...] = jnp.where(lane_u == u, own[:, 0:1], sn[...])
            ss[...] = jnp.where(lane_u == u, own[:, ROWS - 1 : ROWS], ss[...])
        return carry

    lax.fori_loop(0, LEVELS, level, 0)

    @pl.when(is_polar)
    def _():
        tail_row = iota((8, 128), 0)
        d0p = dif[0:1, pl.ds(start, POLAR)]

        def pack(k, carry):
            f, l0 = lax.div(k, 2), 2 * lax.rem(k, 2)
            rows = []
            for p in range(2):
                first = ms[f, l0 + p, 0:1, pl.ds(start, POLAR)]
                last = ms[f, l0 + p, COLS - 1 : COLS, pl.ds(start, POLAR)]
                tail = jnp.where(tail_row == 0, last, jnp.where(tail_row == 1, first, 0.0)) * d0p
                rows += [out[f, l0 + p, :, pl.ds(start, POLAR)], tail]
            turned = jnp.concatenate(rows, 0).T
            pk[k, 0] = turned[:NDEV]
            pk[k, 1] = turned[NDEV:]
            return carry

        lax.fori_loop(0, PAIRS, pack, 0)

    pl.semaphore_wait(barrier, NDEV - 1 + jnp.where(is_polar, 1, 2))

    east_dev, west_dev = lax.rem(me + 1, NDEV), lax.rem(me + NDEV - 1, NDEV)
    to_east = remote(ms.at[:, :, pl.ds(COLS - 1, 1)], hw, s_halo.at[0], r_halo.at[0], la, east_dev)
    to_west = remote(ms.at[:, :, pl.ds(0, 1)], he, s_halo.at[1], r_halo.at[1], la, west_dev)
    to_south = remote(ss, hn, s_halo.at[2], r_halo.at[2], jnp.minimum(la + 1, 3), me)
    to_north = remote(sn, hs, s_halo.at[3], r_halo.at[3], jnp.maximum(la - 1, 0), me)

    size = NDEV // CHUNKS

    def relay(g):
        rows = pl.ds(g * size, size)
        return remote(pk.at[:, 1, rows], rl.at[:, rows], s_rel.at[g], r_rel.at[g], helper_lat, me)

    @pl.when(is_polar)
    def _():
        for g in range(CHUNKS):
            relay(g).start()

    to_east.start()
    to_west.start()
    pl.when(has_south)(to_south.start)
    pl.when(has_north)(to_north.start)

    @pl.when(is_polar)
    def _():
        pltpu.make_async_copy(pk.at[:, 0, mine], arr.at[:, me], r_fwd).start()

        def send(k, carry):
            d = lax.rem(me + k, NDEV)
            remote(pk.at[:, 0, place_of(d)], arr.at[:, me], s_fwd, r_fwd, la, d).start()
            return carry

        lax.fori_loop(1, NDEV, send, 0)

    @pl.when(is_helper)
    def _():
        for g in range(CHUNKS):
            relay(g).wait_recv()

            def send(i, carry, g=g):
                b = lax.rem(i + lax.div(me, CHUNKS), size)
                d = b * CHUNKS + g

                @pl.when(d != me)
                def _():
                    remote(rl.at[:, g * size + b], arr.at[:, me], s_fwd, r_fwd, la, d).start()

                return carry

            lax.fori_loop(0, size, send, 0)
        pltpu.make_async_copy(rl.at[:, mine], arr.at[:, me], r_fwd).start()

    for load in loads[len(early) :]:
        load.wait()

    to_east.wait_recv()
    to_west.wait_recv()
    for f in range(FIELDS):
        for l in range(LEVELS):
            out[f, l, 0:1] += d0 * hw[f, l]
            out[f, l, COLS - 1 : COLS] += d0 * he[f, l]

    @pl.when(has_north)
    def _():
        to_south.wait_recv()
        halo = hn[...]
        d = dif[1:2, 0:128]

        def fix(u, carry):
            f, l = lax.div(u, LEVELS), lax.rem(u, LEVELS)
            value = pltpu.roll(halo, lax.rem(128 - u, 128), 1)
            out[f, l, :, 0:128] += jnp.where(lane_u == 0, d * value, 0.0)
            return carry

        lax.fori_loop(0, FIELDS * LEVELS, fix, 0)

    @pl.when(has_south)
    def _():
        to_north.wait_recv()
        halo = hs[...]
        d = dif[1:2, 128:256]

        def fix(u, carry):
            f, l = lax.div(u, LEVELS), lax.rem(u, LEVELS)
            value = pltpu.roll(halo, 127 - u, 1)
            out[f, l, :, 128:256] += jnp.where(lane_u == 127, d * value, 0.0)
            return carry

        lax.fori_loop(0, FIELDS * LEVELS, fix, 0)

    eye = iota((NDEV, NDEV), 0) == iota((NDEV, NDEV), 1)

    def upright(row):
        return jnp.sum(jnp.where(eye, row.astype(F32), 0.0), axis=1, keepdims=True)

    owner_row = sl[0:1, :].astype(F32)
    owners = upright(owner_row)
    columns, offsets, lengths = (upright(sl[i : i + 1, :]).astype(jnp.int32) for i in range(1, 4))
    before = (owners == owner_row) & (iota((NDEV, NDEV), 1) < iota((NDEV, NDEV), 0))
    rank = jnp.sum(jnp.where(before, 1.0, 0.0), axis=1, keepdims=True)
    slot = rank * NDEV + owners
    twice = iota((NDEV, 128), 0) == lax.rem(iota((NDEV, 128), 1), NDEV)
    slot_row = jnp.sum(jnp.where(twice, slot, 0.0), axis=0, keepdims=True)
    routing = jnp.where(iota((128, 128), 0).astype(F32) == slot_row, 1.0, 0.0).astype(BF16)
    pick = jnp.where(lax.rem(iota((NDEV, 128), 1), NDEV) == columns, 1.0, 0.0).astype(BF16)
    high = offsets >= 128
    inner = lax.rem(offsets, 128)
    lane = iota((NDEV, 128), 1)
    spill = (lane < STRIP) & (inner > 128 - STRIP)
    bits = lax.div(inner, 1)
    zero8 = jnp.zeros((8, ROWS), F32)

    def strips_of(u, carry):
        x = out[lax.div(u, LEVELS), lax.rem(u, LEVELS)]
        top = x.astype(BF16).astype(F32)
        y = dot(pick, jnp.concatenate([top, zero8, x - top, zero8], 0).astype(BF16))
        a = jnp.where(high, y[:, 128:], y[:, :128])
        a = jnp.where(spill, y[:, 128:], a)
        for shift in (64, 32, 16):
            a = jnp.where((bits & shift) != 0, pltpu.roll(a, 128 - shift, 1), a)
        xs[u] = a
        return carry

    lax.fori_loop(0, FIELDS * LEVELS, strips_of, 0)
    window = lax.div(lane, 32)
    for g in range(3):
        both = []
        for h in range(2):
            a = jnp.zeros((NDEV, 128), F32)
            for i in range(4):
                u = 8 * g + 2 * i + h
                if u < FIELDS * LEVELS:
                    v = xs[u] if i == 0 else pltpu.roll(xs[u], 32 * i, 1)
                    a = jnp.where(window == i, v, a)
            for shift in (8, 4, 2, 1):
                a = jnp.where((bits & shift) != 0, pltpu.roll(a, 128 - shift, 1), a)
            both.append(a)
        a = jnp.where(lax.rem(lane, 32) < 16, both[0], pltpu.roll(both[1], 16, 1))
        a = jnp.where(lax.rem(lane, STRIP) < lengths, a, 0.0)
        a = dot(routing, jnp.concatenate(split(a), 0))
        sb[g, 0] = a[:NDEV]
        sb[g, 1] = a[NDEV:]

    pltpu.make_async_copy(sb.at[:, :, me], rb.at[:, :, me], r_nest).start()

    def send_strips(k, carry):
        d = lax.rem(me + k, NDEV)
        remote(sb.at[:, :, d], rb.at[:, :, me], s_nest, r_nest, la, d).start()
        return carry

    lax.fori_loop(1, NDEV, send_strips, 0)

    pltpu.make_async_copy(arr, arr, r_fwd).wait()
    cos, sin = tw[0], tw[1]

    def forward(k, carry):
        hi, lo = split(arr[k])
        y = dot(c1[...], jnp.concatenate([hi, lo, hi], 0))
        re, im = y[:QROWS], y[QROWS:]
        zb[k, :, 0:128] = re * cos + im * sin
        zb[k, :, 128:256] = im * cos - re * sin
        return carry

    lax.fori_loop(0, PAIRS, forward, 0)
    hi, lo = split(zb[...].reshape(PAIRS * QROWS, 256))
    spectrum = dot(jnp.concatenate([hi, lo, hi], 1), b1[...])
    base = jnp.where(la < 2, 0, POLAR) + half * NDEV
    lane_k, q = iota((QROWS, 128), 1), iota((QROWS, 128), 0)
    k1 = lax.rem(lane_k, 32)
    live = (q <= 32) & (k1 < K1)
    keep = live & (jnp.abs(q + 64 * (k1 - 14)) < cut[base + mine])
    spectrum = jnp.where(keep[None], spectrum.reshape(PAIRS, QROWS, 128), 0.0)
    hi, lo = split(spectrum.reshape(PAIRS * QROWS, 128))
    zb[...] = dot(jnp.concatenate([hi, lo, hi], 1), b2[...]).reshape(PAIRS, QROWS, 256)

    def backward(k, carry):
        re, im = zb[k, :, 0:128], zb[k, :, 128:256]
        turned = jnp.concatenate([re * cos - im * sin, re * sin + im * cos], 0)
        hi, lo = split(turned)
        res[k] = dot(c2[...], jnp.concatenate([hi, lo, hi], 0))
        return carry

    lax.fori_loop(0, PAIRS, backward, 0)

    @pl.when(is_polar)
    def _():
        pltpu.make_async_copy(res.at[:, me], ret.at[:, 0, mine], r_ret).start()

    @pl.when(is_helper)
    def _():
        remote(res.at[:, me], ret.at[:, 1, mine], s_ret, r_ret, polar_lat, me).start()

    def send_back(k, carry):
        d = lax.rem(me + k, NDEV)
        remote(res.at[:, d], ret.at[:, half, mine], s_ret, r_ret, polar_lat, d).start()
        return carry

    lax.fori_loop(1, NDEV, send_back, 0)

    pltpu.make_async_copy(rb, rb, r_nest).wait()
    for g in range(3):
        tb[g] = jnp.concatenate([rb[g, 0], rb[g, 1]], 0).T
    for t in range(STRIP):
        x = jnp.concatenate([tb[g, pl.ds(t, 8, stride=STRIP), :] for g in range(3)], 0)
        top = x.astype(BF16).astype(F32)
        lb[:, t * 128 : (t + 1) * 128] = jnp.concatenate([top, x - top], 0).astype(BF16)
    places = npl[0].astype(F32)
    begin = jnp.concatenate([places[0:1], places[1:2]], 1)
    wide = 256
    point = iota((wide, 128), 0).astype(F32)

    def boundary(n, carry):
        first = pl.multiple_of(n * wide, wide)
        away = point + (n * wide).astype(F32) - begin
        hats = []
        for t in range(STRIP):
            d = away - float(RATIO * t)
            hat = jnp.maximum(float(RATIO) - jnp.abs(d), 0.0)
            if t == 0:
                hat = jnp.where(d >= 0.0, hat, 0.0)
            hats.append(hat.astype(BF16))
        total = lax.dot_general(
            lb[...], jnp.concatenate(hats, 1), (((1,), (1,)), ((), ())), preferred_element_type=F32
        )
        total = (total[:24] + total[24:]) * (1.0 / RATIO)
        for f in range(FIELDS):
            nest[0, f, :, pl.ds(first, wide)] = total[f * LEVELS : (f + 1) * LEVELS]
        return carry

    lax.fori_loop(0, NB // wide, boundary, 0)

    @pl.when(is_polar)
    def _():
        pltpu.make_async_copy(ret, ret, r_ret).wait()

        def unpack(k, carry):
            f, l0 = lax.div(k, 2), 2 * lax.rem(k, 2)
            turned = jnp.concatenate([ret[k, 0], ret[k, 1]], 0).T
            out[f, l0, :, pl.ds(start, POLAR)] = turned[:COLS]
            out[f, l0 + 1, :, pl.ds(start, POLAR)] = turned[64 : 64 + COLS]
            return carry

        lax.fori_loop(0, PAIRS, unpack, 0)

    to_east.wait_send()
    to_west.wait_send()
    pl.when(has_south)(to_south.wait_send)
    pl.when(has_north)(to_north.wait_send)
    others = pl.ds(0, NDEV - 1)
    pltpu.make_async_copy(res.at[:, others], res.at[:, others], s_fwd).wait()
    pltpu.make_async_copy(sb.at[:, :, others], sb.at[:, :, others], s_nest).wait()

    @pl.when(is_polar)
    def _():
        for g in range(CHUNKS):
            relay(g).wait_send()
        pltpu.make_async_copy(res.at[:, others], res.at[:, others], s_ret).wait()

    @pl.when(is_helper)
    def _():
        pltpu.make_async_copy(res, res, s_ret).wait()


def local(model_state, diffusion, coupling, cutoff, strip_list, nest_place):
    vmem = pl.BlockSpec(memory_space=pltpu.VMEM)
    hbm = pl.BlockSpec(memory_space=pltpu.HBM)
    dma = pltpu.SemaphoreType.DMA
    args = [
        model_state,
        diffusion,
        jnp.transpose(coupling, (1, 0, 2)),
        cutoff,
        jnp.transpose(strip_list),
        jnp.transpose(nest_place, (0, 2, 1)),
        *[jnp.asarray(t) for t in tables()],
    ]
    spaces = [pltpu.SMEM if i in (2, 3) else pltpu.VMEM for i in range(len(args))]
    return pl.pallas_call(
        step_kernel,
        name="dynamics_step",
        out_shape=[
            jax.ShapeDtypeStruct(model_state.shape, F32),
            jax.ShapeDtypeStruct((1, FIELDS, LEVELS, NB), F32),
        ],
        in_specs=[hbm] * len(args),
        out_specs=[vmem, vmem],
        scratch_shapes=[
            *[space(a.shape, a.dtype) for space, a in zip(spaces, args)],
            dma((len(args),)),
            pltpu.VMEM((PAIRS, 2, NDEV, 128), F32),
            pltpu.VMEM((PAIRS, NDEV, 128), F32),
            pltpu.VMEM((PAIRS, NDEV, 128), F32),
            pltpu.VMEM((PAIRS, NDEV, 128), F32),
            pltpu.VMEM((PAIRS, 2, NDEV, 128), F32),
            pltpu.VMEM((PAIRS, QROWS, 256), F32),
            pltpu.VMEM((COLS, 128), F32),
            pltpu.VMEM((COLS, 128), F32),
            pltpu.VMEM((FIELDS, LEVELS, 1, ROWS), F32),
            pltpu.VMEM((FIELDS, LEVELS, 1, ROWS), F32),
            pltpu.VMEM((COLS, 128), F32),
            pltpu.VMEM((COLS, 128), F32),
            pltpu.VMEM((FIELDS * LEVELS, NDEV, 128), F32),
            pltpu.VMEM((3, 2, NDEV, 128), F32),
            pltpu.VMEM((3, 2, NDEV, 128), F32),
            pltpu.VMEM((3, 128, 128), F32),
            pltpu.VMEM((48, STRIP * 128), BF16),
            dma((CHUNKS,)), dma((CHUNKS,)),
            dma, dma, dma, dma, dma, dma,
            dma((4,)), dma((4,)),
        ],
        compiler_params=pltpu.CompilerParams(
            collective_id=0, has_side_effects=True, vmem_limit_bytes=48 << 20
        ),
    )(*[pltpu.with_memory_space_constraint(a, pltpu.HBM) for a in args])


def solution(mesh):
    return jax.shard_map(
        local,
        mesh=mesh,
        in_specs=(
            P(None, None, "lon", "lat"),
            P(None, "lat"),
            P(),
            P(),
            P(("lat", "lon"), None),
            P(("lat", "lon"), None, None),
        ),
        out_specs=(P(None, None, "lon", "lat"), P(("lat", "lon"), None, None, None)),
        check_vma=False,
    )
```

```python
import jax
import jax.numpy as jnp
import ml_dtypes
import numpy as np
from jax import lax
from jax.experimental import pallas as pl
from jax.experimental.pallas import tpu as pltpu
from jax.sharding import PartitionSpec as P

MESH = pl.DeviceIdType.MESH
F32, BF16 = jnp.float32, jnp.bfloat16
FIELDS, LEVELS, COLS, ROWS = 5, 4, 56, 256
NLON, NDEV, POLAR, NB, RATIO, STRIP = 3584, 64, 128, 2048, 11, 16
PAIRS = FIELDS * LEVELS // 2
QROWS = 40
K1 = 28
NZ = 8


def hi_lo(table):
    hi = table.astype(np.float32).astype(ml_dtypes.bfloat16)
    lo = (table - hi.astype(np.float64)).astype(np.float32).astype(ml_dtypes.bfloat16)
    return hi, lo


def tables():
    q = np.arange(QROWS)
    live = (q <= 32).astype(np.float64)
    c = np.arange(NDEV)
    lane = np.arange(128)
    unit, mu = lane // 64, lane % 64
    m = np.where(mu == 57, -1, mu)
    live_in = (mu <= 57).astype(np.float64)
    live_out = (mu < COLS).astype(np.float64)
    turn = 2 * np.pi * np.outer(q, c) / NDEV
    c1 = np.concatenate([np.cos(turn) * live[:, None], -np.sin(turn) * live[:, None]], 0)
    weight = np.where((q == 0) | (q == 32), 1.0, 2.0) * live / NLON
    c2 = np.concatenate([np.cos(turn) * weight[:, None], -np.sin(turn) * weight[:, None]], 0).T
    phi = 2 * np.pi * np.outer(q, m) / NLON
    twiddle = np.stack([np.cos(phi), np.sin(phi)]) * live[None, :, None]
    out = np.arange(128)
    unit_k, part_k, j = out // 64, (out % 64) // 32, out % 32
    k1 = j - 14
    live_k = (j < K1).astype(np.float64)
    psi = 2 * np.pi * np.outer(m, k1) / COLS
    same = (unit[:, None] == unit_k[None, :]) * live_k[None, :]
    cos, sin = np.cos(psi) * same, np.sin(psi) * same
    real = part_k[None, :] == 0
    b1 = np.concatenate([np.where(real, cos, -sin), np.where(real, sin, cos)], 0)
    b1 = b1 * np.tile(live_in, 2)[:, None]
    b2 = np.concatenate([np.where(real, cos, -sin).T, np.where(real, sin, cos).T], 1)
    b2 = b2 * np.tile(live_out, 2)[None, :]
    def left(t):
        hi, lo = hi_lo(t)
        return np.concatenate([hi, hi, lo], 1)

    def right(t):
        hi, lo = hi_lo(t)
        return np.concatenate([hi, hi, lo], 0)

    return left(c1), twiddle.astype(np.float32), right(b1), right(b2), left(c2)


def split(x):
    hi = x.astype(BF16)
    return hi, (x - hi.astype(F32)).astype(BF16)


def iota(shape, dim):
    return lax.broadcasted_iota(jnp.int32, shape, dim)


def dot(a, b):
    return jnp.dot(a, b, preferred_element_type=F32)


def far_first(step):
    odd = lax.rem(step, 2) == 1
    return jnp.where(odd, 4 - lax.div(step + 1, 2), lax.rem(4 + lax.div(step, 2), NZ))


def peer(me, k):
    last = k >= 56
    side = jnp.where(k < 8, 0, lax.rem(k, 2))
    ring = jnp.where(k < 8, 0, 2 * lax.div(k - 8, 16) + 1 + side)
    inner = jnp.where(k < 8, k, lax.div(lax.rem(k - 8, 16), 2))
    ring = jnp.where(last, NZ - 1, ring)
    inner = 7 - jnp.where(last, k - 56, inner)
    z = lax.rem(lax.div(me, NZ) + far_first(ring), NZ)
    return z * NZ + (lax.rem(me, NZ) ^ inner)


def step_kernel(
    ms_hbm, dif_hbm, coup_hbm, cut_hbm, sl_hbm, npl_hbm, c1_hbm, tw_hbm, b1_hbm, b2_hbm, c2_hbm,
    out, nest,
    ms, dif, coup, cut, sl, npl, c1, tw, b1, b2, c2, s_load,
    pk, rl, arr, res, ret, zb, sn, ss, hw, he, hn, hs, xs, sb, rb, tb, lb,
    s_rel, r_rel, s_fwd, r_fwd, s_ret, r_ret, s_nest, r_nest, s_halo, r_halo,
):
    la, me = lax.axis_index("lat"), lax.axis_index("lon")
    polar_lat = jnp.where(la < 2, 0, 3)
    helper_lat = jnp.where(la < 2, 1, 2)
    is_polar = la == polar_lat
    is_helper = jnp.logical_not(is_polar)
    half = jnp.where(is_polar, 0, 1)
    start = pl.multiple_of(jnp.where(la == 3, ROWS - POLAR, 0), 128)
    has_north, has_south = la > 0, la < 3
    my_z = lax.div(me, NZ)

    def remote(src, dst, s, r, lat, lon):
        return pltpu.make_async_remote_copy(
            src, dst, s, r, device_id={"lat": lat, "lon": lon}, device_id_type=MESH
        )

    early = [(ms_hbm, ms), (dif_hbm, dif), (coup_hbm, coup)]
    late = [(cut_hbm, cut), (sl_hbm, sl), (npl_hbm, npl), (c1_hbm, c1), (tw_hbm, tw)]
    late += [(b1_hbm, b1), (b2_hbm, b2), (c2_hbm, c2)]
    loads = [pltpu.make_async_copy(a, b, s_load.at[i]) for i, (a, b) in enumerate(early + late)]
    for load in loads:
        load.start()

    barrier = pltpu.get_barrier_semaphore()

    def greet(lat, lon):
        pl.semaphore_signal(barrier, device_id={"lat": lat, "lon": lon}, device_id_type=MESH)

    @pl.when(has_north)
    def _():
        greet(la - 1, me)

    @pl.when(has_south)
    def _():
        greet(la + 1, me)

    def greet_plane(k, carry):
        greet(la, peer(me, k))
        return carry

    lax.fori_loop(0, NDEV - 1, greet_plane, 0)
    for load in loads[: len(early)]:
        load.wait()

    d0, d1 = dif[0:1, :], dif[1:2, :]
    lane_row = iota((COLS, ROWS), 1)
    col = iota((COLS, ROWS), 0)
    lane_u = iota((COLS, 128), 1)
    sn[...] = jnp.zeros_like(sn)
    ss[...] = jnp.zeros_like(ss)

    def level(l, carry):
        x = [ms[g, l] for g in range(FIELDS)]
        for f in range(FIELDS):
            own = x[f]
            east = jnp.where(col == COLS - 1, 0.0, pltpu.roll(own, COLS - 1, 0))
            west = jnp.where(col == 0, 0.0, pltpu.roll(own, 1, 0))
            south = jnp.where(lane_row == ROWS - 1, 0.0, pltpu.roll(own, ROWS - 1, 1))
            north = jnp.where(lane_row == 0, 0.0, pltpu.roll(own, 1, 1))
            acc = own + d0 * (east + west - 2.0 * own) + d1 * (north + south - 2.0 * own)
            for g in range(FIELDS):
                acc = acc + coup[f, l, g] * x[g]
            out[f, l] = acc
            u = f * LEVELS + l
            sn[...] = jnp.where(lane_u == u, own[:, 0:1], sn[...])
            ss[...] = jnp.where(lane_u == u, own[:, ROWS - 1 : ROWS], ss[...])
        return carry

    lax.fori_loop(0, LEVELS, level, 0)

    @pl.when(is_polar)
    def _():
        tail_row = iota((8, 128), 0)
        d0p = dif[0:1, pl.ds(start, POLAR)]

        def pack(k, carry):
            f, l0 = lax.div(k, 2), 2 * lax.rem(k, 2)
            rows = []
            for p in range(2):
                first = ms[f, l0 + p, 0:1, pl.ds(start, POLAR)]
                last = ms[f, l0 + p, COLS - 1 : COLS, pl.ds(start, POLAR)]
                tail = jnp.where(tail_row == 0, last, jnp.where(tail_row == 1, first, 0.0)) * d0p
                rows += [out[f, l0 + p, :, pl.ds(start, POLAR)], tail]
            turned = jnp.concatenate(rows, 0).T
            pk[k, 0] = turned[:NDEV]
            pk[k, 1] = turned[NDEV:]
            return carry

        lax.fori_loop(0, PAIRS, pack, 0, unroll=2)

    pl.semaphore_wait(barrier, NDEV - 1 + jnp.where(is_polar, 1, 2))

    east_dev, west_dev = lax.rem(me + 1, NDEV), lax.rem(me + NDEV - 1, NDEV)
    to_east = remote(ms.at[:, :, pl.ds(COLS - 1, 1)], hw, s_halo.at[0], r_halo.at[0], la, east_dev)
    to_west = remote(ms.at[:, :, pl.ds(0, 1)], he, s_halo.at[1], r_halo.at[1], la, west_dev)
    to_south = remote(ss, hn, s_halo.at[2], r_halo.at[2], jnp.minimum(la + 1, 3), me)
    to_north = remote(sn, hs, s_halo.at[3], r_halo.at[3], jnp.maximum(la - 1, 0), me)


    def relay(g):
        rows = pl.ds(lax.rem(my_z + far_first(g), NZ) * NZ, NZ)
        return remote(pk.at[:, 1, rows], rl.at[:, rows], s_rel.at[g], r_rel.at[g], helper_lat, me)

    @pl.when(is_polar)
    def _():
        for g in range(NZ):
            relay(g).start()

    to_east.start()
    to_west.start()
    pl.when(has_south)(to_south.start)
    pl.when(has_north)(to_north.start)

    @pl.when(is_polar)
    def _():
        pltpu.make_async_copy(pk.at[:, 0, me], arr.at[:, me], r_fwd).start()

        def send(k, carry):
            d = peer(me, k)
            remote(pk.at[:, 0, d], arr.at[:, me], s_fwd, r_fwd, la, d).start()
            return carry

        lax.fori_loop(0, NDEV - 1, send, 0)

    @pl.when(is_helper)
    def _():
        for g in range(NZ):
            relay(g).wait_recv()

            def send(i, carry, g=g):
                z = lax.rem(my_z + far_first(g), NZ)
                d = z * NZ + (lax.rem(me, NZ) ^ (7 - i))
                remote(rl.at[:, d], arr.at[:, me], s_fwd, r_fwd, la, d).start()
                return carry

            lax.fori_loop(0, NZ - (g == NZ - 1), send, 0)
        pltpu.make_async_copy(rl.at[:, me], arr.at[:, me], r_fwd).start()

    for load in loads[len(early) :]:
        load.wait()

    to_east.wait_recv()
    to_west.wait_recv()
    for f in range(FIELDS):
        for l in range(LEVELS):
            out[f, l, 0:1] += d0 * hw[f, l]
            out[f, l, COLS - 1 : COLS] += d0 * he[f, l]

    @pl.when(has_north)
    def _():
        to_south.wait_recv()
        halo = hn[...]
        d = dif[1:2, 0:128]

        def fix(u, carry):
            f, l = lax.div(u, LEVELS), lax.rem(u, LEVELS)
            value = pltpu.roll(halo, lax.rem(128 - u, 128), 1)
            out[f, l, :, 0:128] += jnp.where(lane_u == 0, d * value, 0.0)
            return carry

        lax.fori_loop(0, FIELDS * LEVELS, fix, 0, unroll=4)

    @pl.when(has_south)
    def _():
        to_north.wait_recv()
        halo = hs[...]
        d = dif[1:2, 128:256]

        def fix(u, carry):
            f, l = lax.div(u, LEVELS), lax.rem(u, LEVELS)
            value = pltpu.roll(halo, 127 - u, 1)
            out[f, l, :, 128:256] += jnp.where(lane_u == 127, d * value, 0.0)
            return carry

        lax.fori_loop(0, FIELDS * LEVELS, fix, 0, unroll=4)

    eye = iota((NDEV, NDEV), 0) == iota((NDEV, NDEV), 1)

    def upright(row):
        return jnp.sum(jnp.where(eye, row.astype(F32), 0.0), axis=1, keepdims=True)

    owner_row = sl[0:1, :].astype(F32)
    owners = upright(owner_row)
    columns, offsets, lengths = (upright(sl[i : i + 1, :]).astype(jnp.int32) for i in range(1, 4))
    before = (owners == owner_row) & (iota((NDEV, NDEV), 1) < iota((NDEV, NDEV), 0))
    rank = jnp.sum(jnp.where(before, 1.0, 0.0), axis=1, keepdims=True)
    slot = rank * NDEV + owners
    twice = iota((NDEV, 128), 0) == lax.rem(iota((NDEV, 128), 1), NDEV)
    slot_row = jnp.sum(jnp.where(twice, slot, 0.0), axis=0, keepdims=True)
    routing = jnp.where(iota((128, 128), 0).astype(F32) == slot_row, 1.0, 0.0).astype(BF16)
    pick = jnp.where(lax.rem(iota((NDEV, 128), 1), NDEV) == columns, 1.0, 0.0).astype(BF16)
    high = offsets >= 128
    inner = lax.rem(offsets, 128)
    lane = iota((NDEV, 128), 1)
    spill = (lane < STRIP) & (inner > 128 - STRIP)
    bits = lax.div(inner, 1)
    zero8 = jnp.zeros((8, ROWS), F32)

    def strips_of(u, carry):
        x = out[lax.div(u, LEVELS), lax.rem(u, LEVELS)]
        top = x.astype(BF16).astype(F32)
        y = dot(pick, jnp.concatenate([top, zero8, x - top, zero8], 0).astype(BF16))
        a = jnp.where(high, y[:, 128:], y[:, :128])
        a = jnp.where(spill, y[:, 128:], a)
        for shift in (64, 32, 16):
            a = jnp.where((bits & shift) != 0, pltpu.roll(a, 128 - shift, 1), a)
        xs[u] = a
        return carry

    lax.fori_loop(0, FIELDS * LEVELS, strips_of, 0, unroll=4)
    window = lax.div(lane, 32)
    for g in range(3):
        both = []
        for h in range(2):
            a = jnp.zeros((NDEV, 128), F32)
            for i in range(4):
                u = 8 * g + 2 * i + h
                if u < FIELDS * LEVELS:
                    v = xs[u] if i == 0 else pltpu.roll(xs[u], 32 * i, 1)
                    a = jnp.where(window == i, v, a)
            for shift in (8, 4, 2, 1):
                a = jnp.where((bits & shift) != 0, pltpu.roll(a, 128 - shift, 1), a)
            both.append(a)
        a = jnp.where(lax.rem(lane, 32) < 16, both[0], pltpu.roll(both[1], 16, 1))
        a = jnp.where(lax.rem(lane, STRIP) < lengths, a, 0.0)
        a = dot(routing, jnp.concatenate(split(a), 0))
        sb[g, 0] = a[:NDEV]
        sb[g, 1] = a[NDEV:]

    pltpu.make_async_copy(sb.at[:, :, me], rb.at[:, :, me], r_nest).start()

    def send_strips(k, carry):
        d = peer(me, k)
        remote(sb.at[:, :, d], rb.at[:, :, me], s_nest, r_nest, la, d).start()
        return carry

    lax.fori_loop(0, NDEV - 1, send_strips, 0)

    pltpu.make_async_copy(arr, arr, r_fwd).wait()
    cos, sin = tw[0], tw[1]

    def forward(k, carry):
        hi, lo = split(arr[k])
        y = dot(c1[...], jnp.concatenate([hi, lo, hi], 0))
        re, im = y[:QROWS], y[QROWS:]
        zb[k, :, 0:128] = re * cos + im * sin
        zb[k, :, 128:256] = im * cos - re * sin
        return carry

    lax.fori_loop(0, PAIRS, forward, 0, unroll=True)
    hi, lo = split(zb[...].reshape(PAIRS * QROWS, 256))
    spectrum = dot(jnp.concatenate([hi, lo, hi], 1), b1[...])
    base = jnp.where(la < 2, 0, POLAR) + half * NDEV
    lane_k, q = iota((QROWS, 128), 1), iota((QROWS, 128), 0)
    k1 = lax.rem(lane_k, 32)
    live = (q <= 32) & (k1 < K1)
    keep = live & (jnp.abs(q + 64 * (k1 - 14)) < cut[base + me])
    spectrum = jnp.where(keep[None], spectrum.reshape(PAIRS, QROWS, 128), 0.0)
    hi, lo = split(spectrum.reshape(PAIRS * QROWS, 128))
    zb[...] = dot(jnp.concatenate([hi, lo, hi], 1), b2[...]).reshape(PAIRS, QROWS, 256)

    def backward(k, carry):
        re, im = zb[k, :, 0:128], zb[k, :, 128:256]
        turned = jnp.concatenate([re * cos - im * sin, re * sin + im * cos], 0)
        hi, lo = split(turned)
        res[k] = dot(c2[...], jnp.concatenate([hi, lo, hi], 0))
        return carry

    lax.fori_loop(0, PAIRS, backward, 0, unroll=True)

    @pl.when(is_polar)
    def _():
        pltpu.make_async_copy(res.at[:, me], ret.at[:, 0, me], r_ret).start()

    @pl.when(is_helper)
    def _():
        remote(res.at[:, me], ret.at[:, 1, me], s_ret, r_ret, polar_lat, me).start()

    def send_back(k, carry):
        d = peer(me, k)
        remote(res.at[:, d], ret.at[:, half, me], s_ret, r_ret, polar_lat, d).start()
        return carry

    lax.fori_loop(0, NDEV - 1, send_back, 0)

    pltpu.make_async_copy(rb, rb, r_nest).wait()
    for g in range(3):
        tb[g] = jnp.concatenate([rb[g, 0], rb[g, 1]], 0).T
    for t in range(STRIP):
        x = jnp.concatenate([tb[g, pl.ds(t, 8, stride=STRIP), :] for g in range(3)], 0)
        top = x.astype(BF16).astype(F32)
        lb[:, t * 128 : (t + 1) * 128] = jnp.concatenate([top, x - top], 0).astype(BF16)
    places = npl[0].astype(F32)
    begin = jnp.concatenate([places[0:1], places[1:2]], 1)
    wide = 256
    point = iota((wide, 128), 0).astype(F32)

    def boundary(n, carry):
        first = pl.multiple_of(n * wide, wide)
        away = point + (n * wide).astype(F32) - begin
        hats = []
        for t in range(STRIP):
            d = away - float(RATIO * t)
            hat = jnp.maximum(float(RATIO) - jnp.abs(d), 0.0)
            if t == 0:
                hat = jnp.where(d >= 0.0, hat, 0.0)
            hats.append(hat.astype(BF16))
        total = lax.dot_general(
            lb[...], jnp.concatenate(hats, 1), (((1,), (1,)), ((), ())), preferred_element_type=F32
        )
        total = (total[:24] + total[24:]) * (1.0 / RATIO)
        for f in range(FIELDS):
            nest[0, f, :, pl.ds(first, wide)] = total[f * LEVELS : (f + 1) * LEVELS]
        return carry

    lax.fori_loop(0, NB // wide, boundary, 0, unroll=2)

    @pl.when(is_polar)
    def _():
        pltpu.make_async_copy(ret, ret, r_ret).wait()

        def unpack(k, carry):
            f, l0 = lax.div(k, 2), 2 * lax.rem(k, 2)
            turned = jnp.concatenate([ret[k, 0], ret[k, 1]], 0).T
            out[f, l0, :, pl.ds(start, POLAR)] = turned[:COLS]
            out[f, l0 + 1, :, pl.ds(start, POLAR)] = turned[64 : 64 + COLS]
            return carry

        lax.fori_loop(0, PAIRS, unpack, 0, unroll=5)

    to_east.wait_send()
    to_west.wait_send()
    pl.when(has_south)(to_south.wait_send)
    pl.when(has_north)(to_north.wait_send)
    others = pl.ds(0, NDEV - 1)
    pltpu.make_async_copy(res.at[:, others], res.at[:, others], s_fwd).wait()
    pltpu.make_async_copy(sb.at[:, :, others], sb.at[:, :, others], s_nest).wait()

    @pl.when(is_polar)
    def _():
        for g in range(NZ):
            relay(g).wait_send()
        pltpu.make_async_copy(res.at[:, others], res.at[:, others], s_ret).wait()

    @pl.when(is_helper)
    def _():
        pltpu.make_async_copy(res, res, s_ret).wait()


def local(model_state, diffusion, coupling, cutoff, strip_list, nest_place):
    vmem = pl.BlockSpec(memory_space=pltpu.VMEM)
    hbm = pl.BlockSpec(memory_space=pltpu.HBM)
    dma = pltpu.SemaphoreType.DMA
    args = [
        model_state,
        diffusion,
        jnp.transpose(coupling, (1, 0, 2)),
        cutoff,
        jnp.transpose(strip_list),
        jnp.transpose(nest_place, (0, 2, 1)),
        *[jnp.asarray(t) for t in tables()],
    ]
    spaces = [pltpu.SMEM if i in (2, 3) else pltpu.VMEM for i in range(len(args))]
    return pl.pallas_call(
        step_kernel,
        name="dynamics_step",
        out_shape=[
            jax.ShapeDtypeStruct(model_state.shape, F32),
            jax.ShapeDtypeStruct((1, FIELDS, LEVELS, NB), F32),
        ],
        in_specs=[hbm] * len(args),
        out_specs=[vmem, vmem],
        scratch_shapes=[
            *[space(a.shape, a.dtype) for space, a in zip(spaces, args)],
            dma((len(args),)),
            pltpu.VMEM((PAIRS, 2, NDEV, 128), F32),
            pltpu.VMEM((PAIRS, NDEV, 128), F32),
            pltpu.VMEM((PAIRS, NDEV, 128), F32),
            pltpu.VMEM((PAIRS, NDEV, 128), F32),
            pltpu.VMEM((PAIRS, 2, NDEV, 128), F32),
            pltpu.VMEM((PAIRS, QROWS, 256), F32),
            pltpu.VMEM((COLS, 128), F32),
            pltpu.VMEM((COLS, 128), F32),
            pltpu.VMEM((FIELDS, LEVELS, 1, ROWS), F32),
            pltpu.VMEM((FIELDS, LEVELS, 1, ROWS), F32),
            pltpu.VMEM((COLS, 128), F32),
            pltpu.VMEM((COLS, 128), F32),
            pltpu.VMEM((FIELDS * LEVELS, NDEV, 128), F32),
            pltpu.VMEM((3, 2, NDEV, 128), F32),
            pltpu.VMEM((3, 2, NDEV, 128), F32),
            pltpu.VMEM((3, 128, 128), F32),
            pltpu.VMEM((48, STRIP * 128), BF16),
            dma((NZ,)), dma((NZ,)),
            dma, dma, dma, dma, dma, dma,
            dma((4,)), dma((4,)),
        ],
        compiler_params=pltpu.CompilerParams(
            collective_id=0, has_side_effects=True, vmem_limit_bytes=48 << 20
        ),
    )(*[pltpu.with_memory_space_constraint(a, pltpu.HBM) for a in args])


def solution(mesh):
    return jax.shard_map(
        local,
        mesh=mesh,
        in_specs=(
            P(None, None, "lon", "lat"),
            P(None, "lat"),
            P(),
            P(),
            P(("lat", "lon"), None),
            P(("lat", "lon"), None, None),
        ),
        out_specs=(P(None, None, "lon", "lat"), P(("lat", "lon"), None, None, None)),
        check_vma=False,
    )
```

```python
import jax
import jax.numpy as jnp
import ml_dtypes
import numpy as np
from jax import lax
from jax.experimental import pallas as pl
from jax.experimental.pallas import tpu as pltpu
from jax.sharding import PartitionSpec as P

MESH = pl.DeviceIdType.MESH
F32, BF16 = jnp.float32, jnp.bfloat16
FIELDS, LEVELS, COLS, ROWS = 5, 4, 56, 256
NLON, NDEV, POLAR, NB, RATIO, STRIP = 3584, 64, 128, 2048, 11, 16
PAIRS = FIELDS * LEVELS // 2
QROWS = 40
K1 = 28
NZ = 8


def hi_lo(table):
    hi = table.astype(np.float32).astype(ml_dtypes.bfloat16)
    lo = (table - hi.astype(np.float64)).astype(np.float32).astype(ml_dtypes.bfloat16)
    return hi, lo


def tables():
    q = np.arange(QROWS)
    live = (q <= 32).astype(np.float64)
    c = np.arange(NDEV)
    lane = np.arange(128)
    unit, mu = lane // 64, lane % 64
    m = np.where(mu == 57, -1, mu)
    live_in = (mu <= 57).astype(np.float64)
    live_out = (mu < COLS).astype(np.float64)
    turn = 2 * np.pi * np.outer(q, c) / NDEV
    c1 = np.concatenate([np.cos(turn) * live[:, None], -np.sin(turn) * live[:, None]], 0)
    weight = np.where((q == 0) | (q == 32), 1.0, 2.0) * live / NLON
    c2 = np.concatenate([np.cos(turn) * weight[:, None], -np.sin(turn) * weight[:, None]], 0).T
    phi = 2 * np.pi * np.outer(q, m) / NLON
    twiddle = np.stack([np.cos(phi), np.sin(phi)]) * live[None, :, None]
    out = np.arange(128)
    unit_k, part_k, j = out // 64, (out % 64) // 32, out % 32
    k1 = j - 14
    live_k = (j < K1).astype(np.float64)
    psi = 2 * np.pi * np.outer(m, k1) / COLS
    same = (unit[:, None] == unit_k[None, :]) * live_k[None, :]
    cos, sin = np.cos(psi) * same, np.sin(psi) * same
    real = part_k[None, :] == 0
    b1 = np.concatenate([np.where(real, cos, -sin), np.where(real, sin, cos)], 0)
    b1 = b1 * np.tile(live_in, 2)[:, None]
    b2 = np.concatenate([np.where(real, cos, -sin).T, np.where(real, sin, cos).T], 1)
    b2 = b2 * np.tile(live_out, 2)[None, :]
    def left(t):
        hi, lo = hi_lo(t)
        return np.concatenate([hi, hi, lo], 1)

    def right(t):
        hi, lo = hi_lo(t)
        return np.concatenate([hi, hi, lo], 0)

    return left(c1), twiddle.astype(np.float32), right(b1), right(b2), left(c2)


def split(x):
    hi = x.astype(BF16)
    return hi, (x - hi.astype(F32)).astype(BF16)


def iota(shape, dim):
    return lax.broadcasted_iota(jnp.int32, shape, dim)


def dot(a, b):
    return jnp.dot(a, b, preferred_element_type=F32)


def far_first(step):
    odd = lax.rem(step, 2) == 1
    return jnp.where(odd, 4 - lax.div(step + 1, 2), lax.rem(4 + lax.div(step, 2), NZ))


def peer(me, k):
    last = k >= 56
    side = jnp.where(k < 8, 0, lax.rem(k, 2))
    ring = jnp.where(k < 8, 0, 2 * lax.div(k - 8, 16) + 1 + side)
    inner = jnp.where(k < 8, k, lax.div(lax.rem(k - 8, 16), 2))
    ring = jnp.where(last, NZ - 1, ring)
    inner = 7 - jnp.where(last, k - 56, inner)
    z = lax.rem(lax.div(me, NZ) + far_first(ring), NZ)
    return z * NZ + (lax.rem(me, NZ) ^ inner)


def step_kernel(
    ms_hbm, dif_hbm, coup_hbm, cut_hbm, sl_hbm, npl_hbm, c1_hbm, tw_hbm, b1_hbm, b2_hbm, c2_hbm,
    out, nest, ret,
    ms, dif, coup, cut, sl, npl, c1, tw, b1, b2, c2, s_load,
    pk, rl, arr, res, zb, sn, ss, hw, he, hn, hs, xs, sb, rb, tb, lb,
    s_rel, r_rel, s_fwd, r_fwd, s_ret, r_ret, s_nest, r_nest, s_halo, r_halo,
):
    la, me = lax.axis_index("lat"), lax.axis_index("lon")
    polar_lat = jnp.where(la < 2, 0, 3)
    helper_lat = jnp.where(la < 2, 1, 2)
    is_polar = la == polar_lat
    is_helper = jnp.logical_not(is_polar)
    half = jnp.where(is_polar, 0, 1)
    start = pl.multiple_of(jnp.where(la == 3, ROWS - POLAR, 0), 128)
    has_north, has_south = la > 0, la < 3
    my_z = lax.div(me, NZ)

    def remote(src, dst, s, r, lat, lon):
        return pltpu.make_async_remote_copy(
            src, dst, s, r, device_id={"lat": lat, "lon": lon}, device_id_type=MESH
        )

    early = [(ms_hbm, ms), (dif_hbm, dif), (coup_hbm, coup)]
    late = [(cut_hbm, cut), (sl_hbm, sl), (npl_hbm, npl), (c1_hbm, c1), (tw_hbm, tw)]
    late += [(b1_hbm, b1), (b2_hbm, b2), (c2_hbm, c2)]
    loads = [pltpu.make_async_copy(a, b, s_load.at[i]) for i, (a, b) in enumerate(early + late)]
    for load in loads:
        load.start()

    barrier = pltpu.get_barrier_semaphore()

    def greet(lat, lon):
        pl.semaphore_signal(barrier, device_id={"lat": lat, "lon": lon}, device_id_type=MESH)

    @pl.when(has_north)
    def _():
        greet(la - 1, me)

    @pl.when(has_south)
    def _():
        greet(la + 1, me)

    def greet_plane(k, carry):
        greet(la, peer(me, k))
        return carry

    lax.fori_loop(0, NDEV - 1, greet_plane, 0)
    for load in loads[: len(early)]:
        load.wait()

    d0, d1 = dif[0:1, :], dif[1:2, :]
    lane_row = iota((COLS, ROWS), 1)
    col = iota((COLS, ROWS), 0)
    lane_u = iota((COLS, 128), 1)
    sn[...] = jnp.zeros_like(sn)
    ss[...] = jnp.zeros_like(ss)

    def level(l, carry):
        x = [ms[g, l] for g in range(FIELDS)]
        for f in range(FIELDS):
            own = x[f]
            east = jnp.where(col == COLS - 1, 0.0, pltpu.roll(own, COLS - 1, 0))
            west = jnp.where(col == 0, 0.0, pltpu.roll(own, 1, 0))
            south = jnp.where(lane_row == ROWS - 1, 0.0, pltpu.roll(own, ROWS - 1, 1))
            north = jnp.where(lane_row == 0, 0.0, pltpu.roll(own, 1, 1))
            acc = own + d0 * (east + west - 2.0 * own) + d1 * (north + south - 2.0 * own)
            for g in range(FIELDS):
                acc = acc + coup[f, l, g] * x[g]
            out[f, l] = acc
            u = f * LEVELS + l
            sn[...] = jnp.where(lane_u == u, own[:, 0:1], sn[...])
            ss[...] = jnp.where(lane_u == u, own[:, ROWS - 1 : ROWS], ss[...])
        return carry

    lax.fori_loop(0, LEVELS, level, 0)

    @pl.when(is_polar)
    def _():
        tail_row = iota((8, 128), 0)
        d0p = dif[0:1, pl.ds(start, POLAR)]

        def pack(k, carry):
            f, l0 = lax.div(k, 2), 2 * lax.rem(k, 2)
            rows = []
            for p in range(2):
                first = ms[f, l0 + p, 0:1, pl.ds(start, POLAR)]
                last = ms[f, l0 + p, COLS - 1 : COLS, pl.ds(start, POLAR)]
                tail = jnp.where(tail_row == 0, last, jnp.where(tail_row == 1, first, 0.0)) * d0p
                rows += [out[f, l0 + p, :, pl.ds(start, POLAR)], tail]
            turned = jnp.concatenate(rows, 0).T
            pk[k, 0] = turned[:NDEV]
            pk[k, 1] = turned[NDEV:]
            return carry

        lax.fori_loop(0, PAIRS, pack, 0, unroll=2)

    pl.semaphore_wait(barrier, NDEV - 1 + jnp.where(is_polar, 1, 2))

    east_dev, west_dev = lax.rem(me + 1, NDEV), lax.rem(me + NDEV - 1, NDEV)
    to_east = remote(ms.at[:, :, pl.ds(COLS - 1, 1)], hw, s_halo.at[0], r_halo.at[0], la, east_dev)
    to_west = remote(ms.at[:, :, pl.ds(0, 1)], he, s_halo.at[1], r_halo.at[1], la, west_dev)
    to_south = remote(ss, hn, s_halo.at[2], r_halo.at[2], jnp.minimum(la + 1, 3), me)
    to_north = remote(sn, hs, s_halo.at[3], r_halo.at[3], jnp.maximum(la - 1, 0), me)


    def relay(g):
        rows = pl.ds(lax.rem(my_z + far_first(g), NZ) * NZ, NZ)
        return remote(pk.at[:, 1, rows], rl.at[:, rows], s_rel.at[g], r_rel.at[g], helper_lat, me)

    to_east.start()
    to_west.start()
    pl.when(has_south)(to_south.start)
    pl.when(has_north)(to_north.start)

    @pl.when(is_polar)
    def _():
        for g in range(NZ):
            relay(g).start()

    @pl.when(is_polar)
    def _():
        pltpu.make_async_copy(pk.at[:, 0, me], arr.at[:, me], r_fwd).start()

        def send(k, carry):
            d = peer(me, k)
            remote(pk.at[:, 0, d], arr.at[:, me], s_fwd, r_fwd, la, d).start()
            return carry

        lax.fori_loop(0, NDEV - 1, send, 0)

    for load in loads[len(early) :]:
        load.wait()

    eye = iota((NDEV, NDEV), 0) == iota((NDEV, NDEV), 1)

    def upright(row):
        return jnp.sum(jnp.where(eye, row.astype(F32), 0.0), axis=1, keepdims=True)

    owner_row = sl[0:1, :].astype(F32)
    owners = upright(owner_row)
    columns, offsets, lengths = (upright(sl[i : i + 1, :]).astype(jnp.int32) for i in range(1, 4))
    before = (owners == owner_row) & (iota((NDEV, NDEV), 1) < iota((NDEV, NDEV), 0))
    rank = jnp.sum(jnp.where(before, 1.0, 0.0), axis=1, keepdims=True)
    slot = rank * NDEV + owners
    twice = iota((NDEV, 128), 0) == lax.rem(iota((NDEV, 128), 1), NDEV)
    slot_row = jnp.sum(jnp.where(twice, slot, 0.0), axis=0, keepdims=True)
    routing = jnp.where(iota((128, 128), 0).astype(F32) == slot_row, 1.0, 0.0).astype(BF16)
    pick = jnp.where(lax.rem(iota((NDEV, 128), 1), NDEV) == columns, 1.0, 0.0).astype(BF16)
    lane = iota((NDEV, 128), 1)
    high = jnp.broadcast_to(offsets, (NDEV, 128)) >= 128
    inner = lax.rem(offsets, 128)
    spill = (lane < STRIP) & (inner > 128 - STRIP)
    bits = jnp.broadcast_to(inner, (NDEV, 128))
    zero8 = jnp.zeros((8, ROWS), F32)

    to_east.wait_recv()
    to_west.wait_recv()
    for f in range(FIELDS):
        for l in range(LEVELS):
            out[f, l, 0:1] += d0 * hw[f, l]
            out[f, l, COLS - 1 : COLS] += d0 * he[f, l]

    @pl.when(has_north)
    def _():
        to_south.wait_recv()
        halo = hn[...]
        d = dif[1:2, 0:128]

        def fix(u, carry):
            f, l = lax.div(u, LEVELS), lax.rem(u, LEVELS)
            value = pltpu.roll(halo, lax.rem(128 - u, 128), 1)
            out[f, l, :, 0:128] += jnp.where(lane_u == 0, d * value, 0.0)
            return carry

        lax.fori_loop(0, FIELDS * LEVELS, fix, 0, unroll=4)

    @pl.when(has_south)
    def _():
        to_north.wait_recv()
        halo = hs[...]
        d = dif[1:2, 128:256]

        def fix(u, carry):
            f, l = lax.div(u, LEVELS), lax.rem(u, LEVELS)
            value = pltpu.roll(halo, 127 - u, 1)
            out[f, l, :, 128:256] += jnp.where(lane_u == 127, d * value, 0.0)
            return carry

        lax.fori_loop(0, FIELDS * LEVELS, fix, 0, unroll=4)

    def strips_of(u, carry):
        x = out[lax.div(u, LEVELS), lax.rem(u, LEVELS)]
        top = x.astype(BF16).astype(F32)
        y = dot(pick, jnp.concatenate([top, zero8, x - top, zero8], 0).astype(BF16))
        a = jnp.where(high, y[:, 128:], y[:, :128])
        a = jnp.where(spill, y[:, 128:], a)
        for shift in (64, 32, 16):
            a = jnp.where((bits & shift) != 0, pltpu.roll(a, 128 - shift, 1), a)
        xs[u] = a
        return carry

    @pl.when(is_helper)
    def _():
        for g in range(NZ):
            relay(g).wait_recv()

            def send(i, carry, g=g):
                z = lax.rem(my_z + far_first(g), NZ)
                d = z * NZ + (lax.rem(me, NZ) ^ (7 - i))
                remote(rl.at[:, d], arr.at[:, me], s_fwd, r_fwd, la, d).start()
                return carry

            lax.fori_loop(0, NZ - (g == NZ - 1), send, 0)
        pltpu.make_async_copy(rl.at[:, me], arr.at[:, me], r_fwd).start()

    lax.fori_loop(0, FIELDS * LEVELS, strips_of, 0, unroll=4)

    window = lax.div(lane, 32)
    for g in range(3):
        both = []
        for h in range(2):
            a = jnp.zeros((NDEV, 128), F32)
            for i in range(4):
                u = 8 * g + 2 * i + h
                if u < FIELDS * LEVELS:
                    v = xs[u] if i == 0 else pltpu.roll(xs[u], 32 * i, 1)
                    a = jnp.where(window == i, v, a)
            for shift in (8, 4, 2, 1):
                a = jnp.where((bits & shift) != 0, pltpu.roll(a, 128 - shift, 1), a)
            both.append(a)
        a = jnp.where(lax.rem(lane, 32) < 16, both[0], pltpu.roll(both[1], 16, 1))
        a = jnp.where(lax.rem(lane, STRIP) < lengths, a, 0.0)
        a = dot(routing, jnp.concatenate(split(a), 0))
        sb[g, 0] = a[:NDEV]
        sb[g, 1] = a[NDEV:]

    def send_nest():
        pltpu.make_async_copy(sb.at[:, :, me], rb.at[:, :, me], r_nest).start()

        def send(k, carry):
            d = peer(me, k)
            remote(sb.at[:, :, d], rb.at[:, :, me], s_nest, r_nest, la, d).start()
            return carry

        lax.fori_loop(0, NDEV - 1, send, 0)

    send_nest()

    pltpu.make_async_copy(arr, arr, r_fwd).wait()
    cos, sin = tw[0], tw[1]

    def forward(k, carry):
        hi, lo = split(arr[k])
        y = dot(c1[...], jnp.concatenate([hi, lo, hi], 0))
        re, im = y[:QROWS], y[QROWS:]
        zb[k, :, 0:128] = re * cos + im * sin
        zb[k, :, 128:256] = im * cos - re * sin
        return carry

    lax.fori_loop(0, PAIRS, forward, 0, unroll=True)
    hi, lo = split(zb[...].reshape(PAIRS * QROWS, 256))
    spectrum = dot(jnp.concatenate([hi, lo, hi], 1), b1[...])
    base = jnp.where(la < 2, 0, POLAR) + half * NDEV
    lane_k, q = iota((QROWS, 128), 1), iota((QROWS, 128), 0)
    k1 = lax.rem(lane_k, 32)
    live = (q <= 32) & (k1 < K1)
    keep = live & (jnp.abs(q + 64 * (k1 - 14)) < cut[base + me])
    spectrum = jnp.where(keep[None], spectrum.reshape(PAIRS, QROWS, 128), 0.0)
    hi, lo = split(spectrum.reshape(PAIRS * QROWS, 128))
    zb[...] = dot(jnp.concatenate([hi, lo, hi], 1), b2[...]).reshape(PAIRS, QROWS, 256)

    def backward(k, carry):
        re, im = zb[k, :, 0:128], zb[k, :, 128:256]
        turned = jnp.concatenate([re * cos - im * sin, re * sin + im * cos], 0)
        hi, lo = split(turned)
        res[k] = dot(c2[...], jnp.concatenate([hi, lo, hi], 0))
        return carry

    lax.fori_loop(0, PAIRS, backward, 0, unroll=True)

    @pl.when(is_polar)
    def _():
        pltpu.make_async_copy(res.at[:, me], ret.at[:, 0, me], r_ret).start()

    @pl.when(is_helper)
    def _():
        remote(res.at[:, me], ret.at[:, 1, me], s_ret, r_ret, polar_lat, me).start()

    def send_back(k, carry):
        d = peer(me, k)
        remote(res.at[:, d], ret.at[:, half, me], s_ret, r_ret, polar_lat, d).start()
        return carry

    lax.fori_loop(0, NDEV - 1, send_back, 0)

    pltpu.make_async_copy(rb, rb, r_nest).wait()
    for g in range(3):
        tb[g] = jnp.concatenate([rb[g, 0], rb[g, 1]], 0).T
    for t in range(STRIP):
        x = jnp.concatenate([tb[g, pl.ds(t, 8, stride=STRIP), :] for g in range(3)], 0)
        top = x.astype(BF16).astype(F32)
        lb[:, t * 128 : (t + 1) * 128] = jnp.concatenate([top, x - top], 0).astype(BF16)
    places = npl[0].astype(F32)
    begin = jnp.concatenate([places[0:1], places[1:2]], 1)
    wide = 256
    point = iota((wide, 128), 0).astype(F32)

    def boundary(n, carry):
        first = pl.multiple_of(n * wide, wide)
        away = jnp.clip(point + (n * wide).astype(F32) - begin, -32.0, 224.0).astype(BF16)
        hats = []
        for t in range(STRIP):
            d = away - float(RATIO * t)
            hat = jnp.maximum(float(RATIO) - jnp.abs(d), 0.0)
            if t == 0:
                hat = jnp.where(d >= 0.0, hat, jnp.zeros_like(hat))
            hats.append(hat)
        total = lax.dot_general(
            lb[...], jnp.concatenate(hats, 1), (((1,), (1,)), ((), ())), preferred_element_type=F32
        )
        total = (total[:24] + total[24:]) * (1.0 / RATIO)
        for f in range(FIELDS):
            nest[0, f, :, pl.ds(first, wide)] = total[f * LEVELS : (f + 1) * LEVELS]
        return carry

    lax.fori_loop(0, NB // wide, boundary, 0, unroll=2)

    @pl.when(is_polar)
    def _():
        pltpu.make_async_copy(ret, ret, r_ret).wait()

    to_east.wait_send()
    to_west.wait_send()
    pl.when(has_south)(to_south.wait_send)
    pl.when(has_north)(to_north.wait_send)
    others = pl.ds(0, NDEV - 1)
    pltpu.make_async_copy(res.at[:, others], res.at[:, others], s_fwd).wait()
    pltpu.make_async_copy(sb.at[:, :, others], sb.at[:, :, others], s_nest).wait()

    @pl.when(is_polar)
    def _():
        for g in range(NZ):
            relay(g).wait_send()
        pltpu.make_async_copy(res.at[:, others], res.at[:, others], s_ret).wait()

    @pl.when(is_helper)
    def _():
        pltpu.make_async_copy(res, res, s_ret).wait()


def place_kernel(upd, nest, ret, out, nest_out, rows, sem):
    la = lax.axis_index("lat")
    is_polar = (la == 0) | (la == 3)
    start = pl.multiple_of(jnp.where(la == 3, ROWS - POLAR, 0), 128)
    other = pl.multiple_of(ROWS - POLAR - start, 128)
    nest_copy = pltpu.make_async_copy(nest, nest_out, sem.at[0])
    nest_copy.start()

    @pl.when(is_polar)
    def _():
        rest = (slice(None),) * 3 + (pl.ds(other, ROWS - POLAR),)
        rest_copy = pltpu.make_async_copy(upd.at[rest], out.at[rest], sem.at[1])
        rest_copy.start()
        copies = []
        for k in range(PAIRS):
            f, l0 = k // 2, 2 * (k % 2)
            turned = jnp.concatenate([ret[k, 0], ret[k, 1]], 0).T
            rows[f, l0] = turned[:COLS]
            rows[f, l0 + 1] = turned[64 : 64 + COLS]
            pair = pl.ds(l0, 2)
            copies.append(
                pltpu.make_async_copy(
                    rows.at[f, pair], out.at[f, pair, :, pl.ds(start, POLAR)], sem.at[2 + k]
                )
            )
            copies[k].start()
        rest_copy.wait()
        for copy in copies:
            copy.wait()

    @pl.when(jnp.logical_not(is_polar))
    def _():
        whole = pltpu.make_async_copy(upd, out, sem.at[1])
        whole.start()
        whole.wait()

    nest_copy.wait()


def local(model_state, diffusion, coupling, cutoff, strip_list, nest_place):
    vmem = pl.BlockSpec(memory_space=pltpu.VMEM)
    hbm = pl.BlockSpec(memory_space=pltpu.HBM)
    dma = pltpu.SemaphoreType.DMA
    args = [
        model_state,
        diffusion,
        jnp.transpose(coupling, (1, 0, 2)),
        cutoff,
        jnp.transpose(strip_list),
        jnp.transpose(nest_place, (0, 2, 1)),
        *[jnp.asarray(t) for t in tables()],
    ]
    spaces = [pltpu.SMEM if i in (2, 3) else pltpu.VMEM for i in range(len(args))]
    updated, nest, filtered = pl.pallas_call(
        step_kernel,
        name="dynamics_step",
        out_shape=[
            jax.ShapeDtypeStruct(model_state.shape, F32),
            jax.ShapeDtypeStruct((1, FIELDS, LEVELS, NB), F32),
            jax.ShapeDtypeStruct((PAIRS, 2, NDEV, 128), F32),
        ],
        in_specs=[hbm] * len(args),
        out_specs=[vmem, vmem, vmem],
        scratch_shapes=[
            *[space(a.shape, a.dtype) for space, a in zip(spaces, args)],
            dma((len(args),)),
            pltpu.VMEM((PAIRS, 2, NDEV, 128), F32),
            pltpu.VMEM((PAIRS, NDEV, 128), F32),
            pltpu.VMEM((PAIRS, NDEV, 128), F32),
            pltpu.VMEM((PAIRS, NDEV, 128), F32),
            pltpu.VMEM((PAIRS, QROWS, 256), F32),
            pltpu.VMEM((COLS, 128), F32),
            pltpu.VMEM((COLS, 128), F32),
            pltpu.VMEM((FIELDS, LEVELS, 1, ROWS), F32),
            pltpu.VMEM((FIELDS, LEVELS, 1, ROWS), F32),
            pltpu.VMEM((COLS, 128), F32),
            pltpu.VMEM((COLS, 128), F32),
            pltpu.VMEM((FIELDS * LEVELS, NDEV, 128), F32),
            pltpu.VMEM((3, 2, NDEV, 128), F32),
            pltpu.VMEM((3, 2, NDEV, 128), F32),
            pltpu.VMEM((3, 128, 128), F32),
            pltpu.VMEM((48, STRIP * 128), BF16),
            dma((NZ,)), dma((NZ,)),
            dma, dma, dma, dma, dma, dma,
            dma((4,)), dma((4,)),
        ],
        compiler_params=pltpu.CompilerParams(
            collective_id=0, has_side_effects=True, vmem_limit_bytes=48 << 20
        ),
    )(*[pltpu.with_memory_space_constraint(a, pltpu.HBM) for a in args])
    return pl.pallas_call(
        place_kernel,
        name="place_filtered",
        out_shape=[
            jax.ShapeDtypeStruct(updated.shape, F32),
            jax.ShapeDtypeStruct(nest.shape, F32),
        ],
        in_specs=[vmem, vmem, vmem],
        out_specs=[hbm, hbm],
        scratch_shapes=[pltpu.VMEM((FIELDS, LEVELS, COLS, POLAR), F32), dma((2 + PAIRS,))],
        compiler_params=pltpu.CompilerParams(vmem_limit_bytes=16 << 20),
    )(updated, nest, filtered)


def solution(mesh):
    return jax.shard_map(
        local,
        mesh=mesh,
        in_specs=(
            P(None, None, "lon", "lat"),
            P(None, "lat"),
            P(),
            P(),
            P(("lat", "lon"), None),
            P(("lat", "lon"), None, None),
        ),
        out_specs=(P(None, None, "lon", "lat"), P(("lat", "lon"), None, None, None)),
        check_vma=False,
    )
```

```python
import jax
import jax.numpy as jnp
import ml_dtypes
import numpy as np
from jax import lax
from jax.experimental import pallas as pl
from jax.experimental.pallas import tpu as pltpu
from jax.sharding import PartitionSpec as P

MESH = pl.DeviceIdType.MESH
F32, BF16 = jnp.float32, jnp.bfloat16
FIELDS, LEVELS, COLS, ROWS = 5, 4, 56, 256
NLON, NDEV, POLAR, NB, RATIO, STRIP = 3584, 64, 128, 2048, 11, 16
PAIRS = FIELDS * LEVELS // 2
QROWS = 40
K1 = 28
NZ = 8


def hi_lo(table):
    hi = table.astype(np.float32).astype(ml_dtypes.bfloat16)
    lo = (table - hi.astype(np.float64)).astype(np.float32).astype(ml_dtypes.bfloat16)
    return hi, lo


def tables():
    q = np.arange(QROWS)
    live = (q <= 32).astype(np.float64)
    c = np.arange(NDEV)
    lane = np.arange(128)
    unit, mu = lane // 64, lane % 64
    m = np.where(mu == 57, -1, mu)
    live_in = (mu <= 57).astype(np.float64)
    live_out = (mu < COLS).astype(np.float64)
    turn = 2 * np.pi * np.outer(q, c) / NDEV
    c1 = np.concatenate([np.cos(turn) * live[:, None], -np.sin(turn) * live[:, None]], 0)
    weight = np.where((q == 0) | (q == 32), 1.0, 2.0) * live / NLON
    c2 = np.concatenate([np.cos(turn) * weight[:, None], -np.sin(turn) * weight[:, None]], 0).T
    phi = 2 * np.pi * np.outer(q, m) / NLON
    twiddle = np.stack([np.cos(phi), np.sin(phi)]) * live[None, :, None]
    out = np.arange(128)
    unit_k, part_k, j = out // 64, (out % 64) // 32, out % 32
    k1 = j - 14
    live_k = (j < K1).astype(np.float64)
    psi = 2 * np.pi * np.outer(m, k1) / COLS
    same = (unit[:, None] == unit_k[None, :]) * live_k[None, :]
    cos, sin = np.cos(psi) * same, np.sin(psi) * same
    real = part_k[None, :] == 0
    b1 = np.concatenate([np.where(real, cos, -sin), np.where(real, sin, cos)], 0)
    b1 = b1 * np.tile(live_in, 2)[:, None]
    b2 = np.concatenate([np.where(real, cos, -sin).T, np.where(real, sin, cos).T], 1)
    b2 = b2 * np.tile(live_out, 2)[None, :]
    def left(t):
        hi, lo = hi_lo(t)
        return np.concatenate([hi, hi, lo], 1)

    def right(t):
        hi, lo = hi_lo(t)
        return np.concatenate([hi, hi, lo], 0)

    return left(c1), twiddle.astype(np.float32), right(b1), right(b2), left(c2)


def split(x):
    hi = x.astype(BF16)
    return hi, (x - hi.astype(F32)).astype(BF16)


def iota(shape, dim):
    return lax.broadcasted_iota(jnp.int32, shape, dim)


def dot(a, b):
    return jnp.dot(a, b, preferred_element_type=F32)


def far_first(step):
    odd = lax.rem(step, 2) == 1
    return jnp.where(odd, 4 - lax.div(step + 1, 2), lax.rem(4 + lax.div(step, 2), NZ))


def peer(me, k):
    last = k >= 56
    side = jnp.where(k < 8, 0, lax.rem(k, 2))
    ring = jnp.where(k < 8, 0, 2 * lax.div(k - 8, 16) + 1 + side)
    inner = jnp.where(k < 8, k, lax.div(lax.rem(k - 8, 16), 2))
    ring = jnp.where(last, NZ - 1, ring)
    inner = 7 - jnp.where(last, k - 56, inner)
    z = lax.rem(lax.div(me, NZ) + far_first(ring), NZ)
    return z * NZ + (lax.rem(me, NZ) ^ inner)


def step_kernel(
    ms_hbm, dif_hbm, coup_hbm, cut_hbm, sl_hbm, npl_hbm, c1_hbm, tw_hbm, b1_hbm, b2_hbm, c2_hbm,
    out, nest, ret,
    ms, dif, coup, cut, sl, npl, c1, tw, b1, b2, c2, s_load,
    pk, rl, arr, res, zb, sn, ss, hw, he, hn, hs, xs, sb, rb, tb, lb,
    s_rel, r_rel, s_fwd, r_fwd, s_ret, r_ret, s_nest, r_nest, s_halo, r_halo,
):
    la, me = lax.axis_index("lat"), lax.axis_index("lon")
    polar_lat = jnp.where(la < 2, 0, 3)
    helper_lat = jnp.where(la < 2, 1, 2)
    is_polar = la == polar_lat
    is_helper = jnp.logical_not(is_polar)
    half = jnp.where(is_polar, 0, 1)
    start = pl.multiple_of(jnp.where(la == 3, ROWS - POLAR, 0), 128)
    has_north, has_south = la > 0, la < 3
    my_z = lax.div(me, NZ)

    def remote(src, dst, s, r, lat, lon):
        return pltpu.make_async_remote_copy(
            src, dst, s, r, device_id={"lat": lat, "lon": lon}, device_id_type=MESH
        )

    early = [(ms_hbm, ms), (dif_hbm, dif), (coup_hbm, coup)]
    late = [(cut_hbm, cut), (sl_hbm, sl), (npl_hbm, npl), (c1_hbm, c1), (tw_hbm, tw)]
    late += [(b1_hbm, b1), (b2_hbm, b2), (c2_hbm, c2)]
    loads = [pltpu.make_async_copy(a, b, s_load.at[i]) for i, (a, b) in enumerate(early + late)]
    for load in loads:
        load.start()

    barrier = pltpu.get_barrier_semaphore()

    def greet(lat, lon):
        pl.semaphore_signal(barrier, device_id={"lat": lat, "lon": lon}, device_id_type=MESH)

    @pl.when(has_north)
    def _():
        greet(la - 1, me)

    @pl.when(has_south)
    def _():
        greet(la + 1, me)

    def greet_plane(k, carry):
        greet(la, peer(me, k))
        return carry

    lax.fori_loop(0, NDEV - 1, greet_plane, 0)
    for load in loads[: len(early)]:
        load.wait()

    d0, d1 = dif[0:1, :], dif[1:2, :]
    lane_row = iota((COLS, ROWS), 1)
    col = iota((COLS, ROWS), 0)
    lane_u = iota((COLS, 128), 1)
    sn[...] = jnp.zeros_like(sn)
    ss[...] = jnp.zeros_like(ss)

    def level(l, carry):
        x = [ms[g, l] for g in range(FIELDS)]
        for f in range(FIELDS):
            own = x[f]
            east = jnp.where(col == COLS - 1, 0.0, pltpu.roll(own, COLS - 1, 0))
            west = jnp.where(col == 0, 0.0, pltpu.roll(own, 1, 0))
            south = jnp.where(lane_row == ROWS - 1, 0.0, pltpu.roll(own, ROWS - 1, 1))
            north = jnp.where(lane_row == 0, 0.0, pltpu.roll(own, 1, 1))
            acc = own + d0 * (east + west - 2.0 * own) + d1 * (north + south - 2.0 * own)
            for g in range(FIELDS):
                acc = acc + coup[f, l, g] * x[g]
            out[f, l] = acc
            u = f * LEVELS + l
            sn[...] = jnp.where(lane_u == u, own[:, 0:1], sn[...])
            ss[...] = jnp.where(lane_u == u, own[:, ROWS - 1 : ROWS], ss[...])
        return carry

    lax.fori_loop(0, LEVELS, level, 0)

    @pl.when(is_polar)
    def _():
        tail_row = iota((8, 128), 0)
        d0p = dif[0:1, pl.ds(start, POLAR)]

        def pack(k, carry):
            f, l0 = lax.div(k, 2), 2 * lax.rem(k, 2)
            rows = []
            for p in range(2):
                first = ms[f, l0 + p, 0:1, pl.ds(start, POLAR)]
                last = ms[f, l0 + p, COLS - 1 : COLS, pl.ds(start, POLAR)]
                tail = jnp.where(tail_row == 0, last, jnp.where(tail_row == 1, first, 0.0)) * d0p
                rows += [out[f, l0 + p, :, pl.ds(start, POLAR)], tail]
            turned = jnp.concatenate(rows, 0).T
            pk[k, 0] = turned[:NDEV]
            pk[k, 1] = turned[NDEV:]
            return carry

        lax.fori_loop(0, PAIRS, pack, 0, unroll=2)

    pl.semaphore_wait(barrier, NDEV - 1 + jnp.where(is_polar, 1, 2))

    east_dev, west_dev = lax.rem(me + 1, NDEV), lax.rem(me + NDEV - 1, NDEV)
    to_east = remote(ms.at[:, :, pl.ds(COLS - 1, 1)], hw, s_halo.at[0], r_halo.at[0], la, east_dev)
    to_west = remote(ms.at[:, :, pl.ds(0, 1)], he, s_halo.at[1], r_halo.at[1], la, west_dev)
    to_south = remote(ss, hn, s_halo.at[2], r_halo.at[2], jnp.minimum(la + 1, 3), me)
    to_north = remote(sn, hs, s_halo.at[3], r_halo.at[3], jnp.maximum(la - 1, 0), me)


    def relay(g):
        rows = pl.ds(lax.rem(my_z + far_first(g), NZ) * NZ, NZ)
        return remote(pk.at[:, 1, rows], rl.at[:, rows], s_rel.at[g], r_rel.at[g], helper_lat, me)

    to_east.start()
    to_west.start()
    pl.when(has_south)(to_south.start)
    pl.when(has_north)(to_north.start)

    @pl.when(is_polar)
    def _():
        for g in range(NZ):
            relay(g).start()

    @pl.when(is_polar)
    def _():
        pltpu.make_async_copy(pk.at[:, 0, me], arr.at[:, me], r_fwd).start()

        def send(k, carry):
            d = peer(me, k)
            remote(pk.at[:, 0, d], arr.at[:, me], s_fwd, r_fwd, la, d).start()
            return carry

        lax.fori_loop(0, NDEV - 1, send, 0)

    for load in loads[len(early) :]:
        load.wait()

    eye = iota((NDEV, NDEV), 0) == iota((NDEV, NDEV), 1)

    def upright(row):
        return jnp.sum(jnp.where(eye, row.astype(F32), 0.0), axis=1, keepdims=True)

    owner_row = sl[0:1, :].astype(F32)
    owners = upright(owner_row)
    columns, offsets, lengths = (upright(sl[i : i + 1, :]).astype(jnp.int32) for i in range(1, 4))
    before = (owners == owner_row) & (iota((NDEV, NDEV), 1) < iota((NDEV, NDEV), 0))
    rank = jnp.sum(jnp.where(before, 1.0, 0.0), axis=1, keepdims=True)
    slot = rank * NDEV + owners
    twice = iota((NDEV, 128), 0) == lax.rem(iota((NDEV, 128), 1), NDEV)
    slot_row = jnp.sum(jnp.where(twice, slot, 0.0), axis=0, keepdims=True)
    routing = jnp.where(iota((128, 128), 0).astype(F32) == slot_row, 1.0, 0.0).astype(BF16)
    pick = jnp.where(lax.rem(iota((NDEV, 128), 1), NDEV) == columns, 1.0, 0.0).astype(BF16)
    lane = iota((NDEV, 128), 1)
    high = jnp.broadcast_to(offsets, (NDEV, 128)) >= 128
    inner = lax.rem(offsets, 128)
    spill = (lane < STRIP) & (inner > 128 - STRIP)
    bits = jnp.broadcast_to(inner, (NDEV, 128))
    zero8 = jnp.zeros((8, ROWS), F32)

    def fix_lon():
        to_east.wait_recv()
        to_west.wait_recv()
        for f in range(FIELDS):
            for l in range(LEVELS):
                out[f, l, 0:1] += d0 * hw[f, l]
                out[f, l, COLS - 1 : COLS] += d0 * he[f, l]

    def fix_lat(copy, buffer, tile, row):
        copy.wait_recv()
        halo = buffer[...]
        d = dif[1:2, tile : tile + 128]

        def fix(u, carry):
            f, l = lax.div(u, LEVELS), lax.rem(u, LEVELS)
            value = pltpu.roll(halo, lax.rem(128 + row - u, 128), 1)
            out[f, l, :, tile : tile + 128] += jnp.where(lane_u == row, d * value, 0.0)
            return carry

        lax.fori_loop(0, FIELDS * LEVELS, fix, 0, unroll=4)

    def fix_north():
        fix_lat(to_south, hn, 0, 0)

    def fix_south():
        fix_lat(to_north, hs, 128, 127)

    def strips_of(u, carry):
        x = out[lax.div(u, LEVELS), lax.rem(u, LEVELS)]
        top = x.astype(BF16).astype(F32)
        y = dot(pick, jnp.concatenate([top, zero8, x - top, zero8], 0).astype(BF16))
        a = jnp.where(high, y[:, 128:], y[:, :128])
        a = jnp.where(spill, y[:, 128:], a)
        for shift in (64, 32, 16):
            a = jnp.where((bits & shift) != 0, pltpu.roll(a, 128 - shift, 1), a)
        xs[u] = a
        return carry

    def cut_strips(first, last):
        lax.fori_loop(first, last, strips_of, 0, unroll=4)

    @pl.when(is_helper)
    def _():
        between = {
            0: fix_lon, 1: fix_north, 2: fix_south,
            3: lambda: cut_strips(0, 4), 4: lambda: cut_strips(4, 8), 5: lambda: cut_strips(8, 12), 6: lambda: cut_strips(12, 16)
        }
        for g in range(NZ):
            relay(g).wait_recv()

            def send(i, carry, g=g):
                z = lax.rem(my_z + far_first(g), NZ)
                d = z * NZ + (lax.rem(me, NZ) ^ (7 - i))
                remote(rl.at[:, d], arr.at[:, me], s_fwd, r_fwd, la, d).start()
                return carry

            lax.fori_loop(0, NZ - (g == NZ - 1), send, 0)
            if g in between:
                between[g]()
        pltpu.make_async_copy(rl.at[:, me], arr.at[:, me], r_fwd).start()
        cut_strips(16, FIELDS * LEVELS)

    @pl.when(is_polar)
    def _():
        fix_lon()
        pl.when(has_north)(fix_north)
        pl.when(has_south)(fix_south)
        cut_strips(0, FIELDS * LEVELS)

    window = lax.div(lane, 32)
    for g in range(3):
        both = []
        for h in range(2):
            a = jnp.zeros((NDEV, 128), F32)
            for i in range(4):
                u = 8 * g + 2 * i + h
                if u < FIELDS * LEVELS:
                    v = xs[u] if i == 0 else pltpu.roll(xs[u], 32 * i, 1)
                    a = jnp.where(window == i, v, a)
            for shift in (8, 4, 2, 1):
                a = jnp.where((bits & shift) != 0, pltpu.roll(a, 128 - shift, 1), a)
            both.append(a)
        a = jnp.where(lax.rem(lane, 32) < 16, both[0], pltpu.roll(both[1], 16, 1))
        a = jnp.where(lax.rem(lane, STRIP) < lengths, a, 0.0)
        a = dot(routing, jnp.concatenate(split(a), 0))
        sb[g, 0] = a[:NDEV]
        sb[g, 1] = a[NDEV:]

    def send_nest():
        pltpu.make_async_copy(sb.at[:, :, me], rb.at[:, :, me], r_nest).start()

        def send(k, carry):
            d = peer(me, k)
            remote(sb.at[:, :, d], rb.at[:, :, me], s_nest, r_nest, la, d).start()
            return carry

        lax.fori_loop(0, NDEV - 1, send, 0)

    send_nest()

    pltpu.make_async_copy(arr, arr, r_fwd).wait()
    cos, sin = tw[0], tw[1]

    def forward(k, carry):
        hi, lo = split(arr[k])
        y = dot(c1[...], jnp.concatenate([hi, lo, hi], 0))
        re, im = y[:QROWS], y[QROWS:]
        zb[k, :, 0:128] = re * cos + im * sin
        zb[k, :, 128:256] = im * cos - re * sin
        return carry

    lax.fori_loop(0, PAIRS, forward, 0, unroll=True)
    hi, lo = split(zb[...].reshape(PAIRS * QROWS, 256))
    spectrum = dot(jnp.concatenate([hi, lo, hi], 1), b1[...])
    base = jnp.where(la < 2, 0, POLAR) + half * NDEV
    lane_k, q = iota((QROWS, 128), 1), iota((QROWS, 128), 0)
    k1 = lax.rem(lane_k, 32)
    live = (q <= 32) & (k1 < K1)
    keep = live & (jnp.abs(q + 64 * (k1 - 14)) < cut[base + me])
    spectrum = jnp.where(keep[None], spectrum.reshape(PAIRS, QROWS, 128), 0.0)
    hi, lo = split(spectrum.reshape(PAIRS * QROWS, 128))
    zb[...] = dot(jnp.concatenate([hi, lo, hi], 1), b2[...]).reshape(PAIRS, QROWS, 256)

    def backward(k, carry):
        re, im = zb[k, :, 0:128], zb[k, :, 128:256]
        turned = jnp.concatenate([re * cos - im * sin, re * sin + im * cos], 0)
        hi, lo = split(turned)
        res[k] = dot(c2[...], jnp.concatenate([hi, lo, hi], 0))
        return carry

    lax.fori_loop(0, PAIRS, backward, 0, unroll=True)

    @pl.when(is_polar)
    def _():
        pltpu.make_async_copy(res.at[:, me], ret.at[:, 0, me], r_ret).start()

    @pl.when(is_helper)
    def _():
        remote(res.at[:, me], ret.at[:, 1, me], s_ret, r_ret, polar_lat, me).start()

    def send_back(k, carry):
        d = peer(me, k)
        remote(res.at[:, d], ret.at[:, half, me], s_ret, r_ret, polar_lat, d).start()
        return carry

    lax.fori_loop(0, NDEV - 1, send_back, 0)

    pltpu.make_async_copy(rb, rb, r_nest).wait()
    for g in range(3):
        tb[g] = jnp.concatenate([rb[g, 0], rb[g, 1]], 0).T
    for t in range(STRIP):
        x = jnp.concatenate([tb[g, pl.ds(t, 8, stride=STRIP), :] for g in range(3)], 0)
        top = x.astype(BF16).astype(F32)
        lb[:, t * 128 : (t + 1) * 128] = jnp.concatenate([top, x - top], 0).astype(BF16)
    places = npl[0].astype(F32)
    begin = jnp.concatenate([places[0:1], places[1:2]], 1)
    wide = 256
    point = iota((wide, 128), 0).astype(F32)

    def boundary(n, carry):
        first = pl.multiple_of(n * wide, wide)
        away = jnp.clip(point + (n * wide).astype(F32) - begin, -32.0, 224.0).astype(BF16)
        hats = []
        for t in range(STRIP):
            d = away - float(RATIO * t)
            hat = jnp.maximum(float(RATIO) - jnp.abs(d), 0.0)
            if t == 0:
                hat = jnp.where(d >= 0.0, hat, jnp.zeros_like(hat))
            hats.append(hat)
        total = lax.dot_general(
            lb[...], jnp.concatenate(hats, 1), (((1,), (1,)), ((), ())), preferred_element_type=F32
        )
        total = (total[:24] + total[24:]) * (1.0 / RATIO)
        for f in range(FIELDS):
            nest[0, f, :, pl.ds(first, wide)] = total[f * LEVELS : (f + 1) * LEVELS]
        return carry

    lax.fori_loop(0, NB // wide, boundary, 0, unroll=2)

    @pl.when(is_polar)
    def _():
        pltpu.make_async_copy(ret, ret, r_ret).wait()

    to_east.wait_send()
    to_west.wait_send()
    pl.when(has_south)(to_south.wait_send)
    pl.when(has_north)(to_north.wait_send)
    others = pl.ds(0, NDEV - 1)
    pltpu.make_async_copy(res.at[:, others], res.at[:, others], s_fwd).wait()
    pltpu.make_async_copy(sb.at[:, :, others], sb.at[:, :, others], s_nest).wait()

    @pl.when(is_polar)
    def _():
        for g in range(NZ):
            relay(g).wait_send()
        pltpu.make_async_copy(res.at[:, others], res.at[:, others], s_ret).wait()

    @pl.when(is_helper)
    def _():
        pltpu.make_async_copy(res, res, s_ret).wait()


def place_kernel(upd, nest, ret, out, nest_out, rows, sem):
    la = lax.axis_index("lat")
    is_polar = (la == 0) | (la == 3)
    start = pl.multiple_of(jnp.where(la == 3, ROWS - POLAR, 0), 128)
    other = pl.multiple_of(ROWS - POLAR - start, 128)
    nest_copy = pltpu.make_async_copy(nest, nest_out, sem.at[0])
    nest_copy.start()

    @pl.when(is_polar)
    def _():
        rest = (slice(None),) * 3 + (pl.ds(other, ROWS - POLAR),)
        rest_copy = pltpu.make_async_copy(upd.at[rest], out.at[rest], sem.at[1])
        rest_copy.start()
        copies = []
        for k in range(PAIRS):
            f, l0 = k // 2, 2 * (k % 2)
            turned = jnp.concatenate([ret[k, 0], ret[k, 1]], 0).T
            rows[f, l0] = turned[:COLS]
            rows[f, l0 + 1] = turned[64 : 64 + COLS]
            pair = pl.ds(l0, 2)
            copies.append(
                pltpu.make_async_copy(
                    rows.at[f, pair], out.at[f, pair, :, pl.ds(start, POLAR)], sem.at[2 + k]
                )
            )
            copies[k].start()
        rest_copy.wait()
        for copy in copies:
            copy.wait()

    @pl.when(jnp.logical_not(is_polar))
    def _():
        whole = pltpu.make_async_copy(upd, out, sem.at[1])
        whole.start()
        whole.wait()

    nest_copy.wait()


def local(model_state, diffusion, coupling, cutoff, strip_list, nest_place):
    vmem = pl.BlockSpec(memory_space=pltpu.VMEM)
    hbm = pl.BlockSpec(memory_space=pltpu.HBM)
    dma = pltpu.SemaphoreType.DMA
    args = [
        model_state,
        diffusion,
        jnp.transpose(coupling, (1, 0, 2)),
        cutoff,
        jnp.transpose(strip_list),
        jnp.transpose(nest_place, (0, 2, 1)),
        *[jnp.asarray(t) for t in tables()],
    ]
    spaces = [pltpu.SMEM if i in (2, 3) else pltpu.VMEM for i in range(len(args))]
    updated, nest, filtered = pl.pallas_call(
        step_kernel,
        name="dynamics_step",
        out_shape=[
            jax.ShapeDtypeStruct(model_state.shape, F32),
            jax.ShapeDtypeStruct((1, FIELDS, LEVELS, NB), F32),
            jax.ShapeDtypeStruct((PAIRS, 2, NDEV, 128), F32),
        ],
        in_specs=[hbm] * len(args),
        out_specs=[vmem, vmem, vmem],
        scratch_shapes=[
            *[space(a.shape, a.dtype) for space, a in zip(spaces, args)],
            dma((len(args),)),
            pltpu.VMEM((PAIRS, 2, NDEV, 128), F32),
            pltpu.VMEM((PAIRS, NDEV, 128), F32),
            pltpu.VMEM((PAIRS, NDEV, 128), F32),
            pltpu.VMEM((PAIRS, NDEV, 128), F32),
            pltpu.VMEM((PAIRS, QROWS, 256), F32),
            pltpu.VMEM((COLS, 128), F32),
            pltpu.VMEM((COLS, 128), F32),
            pltpu.VMEM((FIELDS, LEVELS, 1, ROWS), F32),
            pltpu.VMEM((FIELDS, LEVELS, 1, ROWS), F32),
            pltpu.VMEM((COLS, 128), F32),
            pltpu.VMEM((COLS, 128), F32),
            pltpu.VMEM((FIELDS * LEVELS, NDEV, 128), F32),
            pltpu.VMEM((3, 2, NDEV, 128), F32),
            pltpu.VMEM((3, 2, NDEV, 128), F32),
            pltpu.VMEM((3, 128, 128), F32),
            pltpu.VMEM((48, STRIP * 128), BF16),
            dma((NZ,)), dma((NZ,)),
            dma, dma, dma, dma, dma, dma,
            dma((4,)), dma((4,)),
        ],
        compiler_params=pltpu.CompilerParams(
            collective_id=0, has_side_effects=True, vmem_limit_bytes=48 << 20
        ),
    )(*[pltpu.with_memory_space_constraint(a, pltpu.HBM) for a in args])
    return pl.pallas_call(
        place_kernel,
        name="place_filtered",
        out_shape=[
            jax.ShapeDtypeStruct(updated.shape, F32),
            jax.ShapeDtypeStruct(nest.shape, F32),
        ],
        in_specs=[vmem, vmem, vmem],
        out_specs=[hbm, hbm],
        scratch_shapes=[pltpu.VMEM((FIELDS, LEVELS, COLS, POLAR), F32), dma((2 + PAIRS,))],
        compiler_params=pltpu.CompilerParams(vmem_limit_bytes=16 << 20),
    )(updated, nest, filtered)


def solution(mesh):
    return jax.shard_map(
        local,
        mesh=mesh,
        in_specs=(
            P(None, None, "lon", "lat"),
            P(None, "lat"),
            P(),
            P(),
            P(("lat", "lon"), None),
            P(("lat", "lon"), None, None),
        ),
        out_specs=(P(None, None, "lon", "lat"), P(("lat", "lon"), None, None, None)),
        check_vma=False,
    )
```

```python
import jax
import jax.numpy as jnp
import ml_dtypes
import numpy as np
from jax import lax
from jax.experimental import pallas as pl
from jax.experimental.pallas import tpu as pltpu
from jax.sharding import PartitionSpec as P

MESH = pl.DeviceIdType.MESH
F32, BF16 = jnp.float32, jnp.bfloat16
FIELDS, LEVELS, COLS, ROWS = 5, 4, 56, 256
NLON, NDEV, POLAR, NB, RATIO, STRIP = 3584, 64, 128, 2048, 11, 16
PAIRS = FIELDS * LEVELS // 2
PARTS = 2
SIZE = PAIRS // PARTS
QROWS = 40
K1 = 28
NZ = 8


def hi_lo(table):
    hi = table.astype(np.float32).astype(ml_dtypes.bfloat16)
    lo = (table - hi.astype(np.float64)).astype(np.float32).astype(ml_dtypes.bfloat16)
    return hi, lo


def tables():
    q = np.arange(QROWS)
    live = (q <= 32).astype(np.float64)
    c = np.arange(NDEV)
    lane = np.arange(128)
    unit, mu = lane // 64, lane % 64
    m = np.where(mu == 57, -1, mu)
    live_in = (mu <= 57).astype(np.float64)
    live_out = (mu < COLS).astype(np.float64)
    turn = 2 * np.pi * np.outer(q, c) / NDEV
    c1 = np.concatenate([np.cos(turn) * live[:, None], -np.sin(turn) * live[:, None]], 0)
    weight = np.where((q == 0) | (q == 32), 1.0, 2.0) * live / NLON
    c2 = np.concatenate([np.cos(turn) * weight[:, None], -np.sin(turn) * weight[:, None]], 0).T
    phi = 2 * np.pi * np.outer(q, m) / NLON
    twiddle = np.stack([np.cos(phi), np.sin(phi)]) * live[None, :, None]
    out = np.arange(128)
    unit_k, part_k, j = out // 64, (out % 64) // 32, out % 32
    k1 = j - 14
    live_k = (j < K1).astype(np.float64)
    psi = 2 * np.pi * np.outer(m, k1) / COLS
    same = (unit[:, None] == unit_k[None, :]) * live_k[None, :]
    cos, sin = np.cos(psi) * same, np.sin(psi) * same
    real = part_k[None, :] == 0
    b1 = np.concatenate([np.where(real, cos, -sin), np.where(real, sin, cos)], 0)
    b1 = b1 * np.tile(live_in, 2)[:, None]
    b2 = np.concatenate([np.where(real, cos, -sin).T, np.where(real, sin, cos).T], 1)
    b2 = b2 * np.tile(live_out, 2)[None, :]
    def left(t):
        hi, lo = hi_lo(t)
        return np.concatenate([hi, hi, lo], 1)

    def right(t):
        hi, lo = hi_lo(t)
        return np.concatenate([hi, hi, lo], 0)

    return left(c1), twiddle.astype(np.float32), right(b1), right(b2), left(c2)


def split(x):
    hi = x.astype(BF16)
    return hi, (x - hi.astype(F32)).astype(BF16)


def iota(shape, dim):
    return lax.broadcasted_iota(jnp.int32, shape, dim)


def dot(a, b):
    return jnp.dot(a, b, preferred_element_type=F32)


def far_first(step):
    odd = lax.rem(step, 2) == 1
    return jnp.where(odd, 4 - lax.div(step + 1, 2), lax.rem(4 + lax.div(step, 2), NZ))


def peer(me, k):
    last = k >= 56
    side = jnp.where(k < 8, 0, lax.rem(k, 2))
    ring = jnp.where(k < 8, 0, 2 * lax.div(k - 8, 16) + 1 + side)
    inner = jnp.where(k < 8, k, lax.div(lax.rem(k - 8, 16), 2))
    ring = jnp.where(last, NZ - 1, ring)
    inner = 7 - jnp.where(last, k - 56, inner)
    z = lax.rem(lax.div(me, NZ) + far_first(ring), NZ)
    return z * NZ + (lax.rem(me, NZ) ^ inner)


def step_kernel(
    ms_hbm, dif_hbm, coup_hbm, cut_hbm, sl_hbm, npl_hbm, c1_hbm, tw_hbm, b1_hbm, b2_hbm, c2_hbm,
    out, nest, ret,
    ms, dif, coup, cut, sl, npl, c1, tw, b1, b2, c2, s_load,
    pk, rl, arr, res, zb, sn, ss, hw, he, hn, hs, xs, sb, rb, tb, lb,
    s_rel, r_rel, s_fwd, r_fwd, s_ret, r_ret, s_nest, r_nest, s_halo, r_halo,
):
    la, me = lax.axis_index("lat"), lax.axis_index("lon")
    polar_lat = jnp.where(la < 2, 0, 3)
    helper_lat = jnp.where(la < 2, 1, 2)
    is_polar = la == polar_lat
    is_helper = jnp.logical_not(is_polar)
    half = jnp.where(is_polar, 0, 1)
    start = pl.multiple_of(jnp.where(la == 3, ROWS - POLAR, 0), 128)
    has_north, has_south = la > 0, la < 3
    my_z = lax.div(me, NZ)

    def remote(src, dst, s, r, lat, lon):
        return pltpu.make_async_remote_copy(
            src, dst, s, r, device_id={"lat": lat, "lon": lon}, device_id_type=MESH
        )

    early = [(ms_hbm, ms), (dif_hbm, dif), (coup_hbm, coup)]
    late = [(cut_hbm, cut), (sl_hbm, sl), (npl_hbm, npl), (c1_hbm, c1), (tw_hbm, tw)]
    late += [(b1_hbm, b1), (b2_hbm, b2), (c2_hbm, c2)]
    loads = [pltpu.make_async_copy(a, b, s_load.at[i]) for i, (a, b) in enumerate(early + late)]
    for load in loads:
        load.start()

    barrier = pltpu.get_barrier_semaphore()

    def greet(lat, lon):
        pl.semaphore_signal(barrier, device_id={"lat": lat, "lon": lon}, device_id_type=MESH)

    @pl.when(has_north)
    def _():
        greet(la - 1, me)

    @pl.when(has_south)
    def _():
        greet(la + 1, me)

    def greet_plane(k, carry):
        greet(la, peer(me, k))
        return carry

    lax.fori_loop(0, NDEV - 1, greet_plane, 0)
    for load in loads[: len(early)]:
        load.wait()

    d0, d1 = dif[0:1, :], dif[1:2, :]
    lane_row = iota((COLS, ROWS), 1)
    col = iota((COLS, ROWS), 0)
    lane_u = iota((COLS, 128), 1)
    sn[...] = jnp.zeros_like(sn)
    ss[...] = jnp.zeros_like(ss)

    def level(l, carry):
        x = [ms[g, l] for g in range(FIELDS)]
        for f in range(FIELDS):
            own = x[f]
            east = jnp.where(col == COLS - 1, 0.0, pltpu.roll(own, COLS - 1, 0))
            west = jnp.where(col == 0, 0.0, pltpu.roll(own, 1, 0))
            south = jnp.where(lane_row == ROWS - 1, 0.0, pltpu.roll(own, ROWS - 1, 1))
            north = jnp.where(lane_row == 0, 0.0, pltpu.roll(own, 1, 1))
            acc = own + d0 * (east + west - 2.0 * own) + d1 * (north + south - 2.0 * own)
            for g in range(FIELDS):
                acc = acc + coup[f, l, g] * x[g]
            out[f, l] = acc
            u = f * LEVELS + l
            sn[...] = jnp.where(lane_u == u, own[:, 0:1], sn[...])
            ss[...] = jnp.where(lane_u == u, own[:, ROWS - 1 : ROWS], ss[...])
        return carry

    lax.fori_loop(0, LEVELS, level, 0)

    @pl.when(is_polar)
    def _():
        tail_row = iota((8, 128), 0)
        d0p = dif[0:1, pl.ds(start, POLAR)]

        def pack(k, carry):
            f, l0 = lax.div(k, 2), 2 * lax.rem(k, 2)
            rows = []
            for p in range(2):
                first = ms[f, l0 + p, 0:1, pl.ds(start, POLAR)]
                last = ms[f, l0 + p, COLS - 1 : COLS, pl.ds(start, POLAR)]
                tail = jnp.where(tail_row == 0, last, jnp.where(tail_row == 1, first, 0.0)) * d0p
                rows += [out[f, l0 + p, :, pl.ds(start, POLAR)], tail]
            turned = jnp.concatenate(rows, 0).T
            pk[k, 0] = turned[:NDEV]
            pk[k, 1] = turned[NDEV:]
            return carry

        lax.fori_loop(0, PAIRS, pack, 0, unroll=2)

    pl.semaphore_wait(barrier, NDEV - 1 + jnp.where(is_polar, 1, 2))

    east_dev, west_dev = lax.rem(me + 1, NDEV), lax.rem(me + NDEV - 1, NDEV)
    to_east = remote(ms.at[:, :, pl.ds(COLS - 1, 1)], hw, s_halo.at[0], r_halo.at[0], la, east_dev)
    to_west = remote(ms.at[:, :, pl.ds(0, 1)], he, s_halo.at[1], r_halo.at[1], la, west_dev)
    to_south = remote(ss, hn, s_halo.at[2], r_halo.at[2], jnp.minimum(la + 1, 3), me)
    to_north = remote(sn, hs, s_halo.at[3], r_halo.at[3], jnp.maximum(la - 1, 0), me)


    def relay(part, g):
        rows = pl.ds(lax.rem(my_z + far_first(g), NZ) * NZ, NZ)
        pairs, i = pl.ds(part * SIZE, SIZE), part * NZ + g
        return remote(
            pk.at[pairs, 1, rows], rl.at[pairs, rows], s_rel.at[i], r_rel.at[i], helper_lat, me
        )

    to_east.start()
    to_west.start()
    pl.when(has_south)(to_south.start)
    pl.when(has_north)(to_north.start)

    @pl.when(is_polar)
    def _():
        for part in range(PARTS):
            for g in range(NZ):
                relay(part, g).start()

    @pl.when(is_polar)
    def _():
        for part in range(PARTS):
            pairs, s, r = pl.ds(part * SIZE, SIZE), s_fwd.at[part], r_fwd.at[part]
            pltpu.make_async_copy(pk.at[pairs, 0, me], arr.at[pairs, me], r).start()

            def send(k, carry, pairs=pairs, s=s, r=r):
                d = peer(me, k)
                remote(pk.at[pairs, 0, d], arr.at[pairs, me], s, r, la, d).start()
                return carry

            lax.fori_loop(0, NDEV - 1, send, 0)

    for load in loads[len(early) :]:
        load.wait()

    eye = iota((NDEV, NDEV), 0) == iota((NDEV, NDEV), 1)

    def upright(row):
        return jnp.sum(jnp.where(eye, row.astype(F32), 0.0), axis=1, keepdims=True)

    owner_row = sl[0:1, :].astype(F32)
    owners = upright(owner_row)
    columns, offsets, lengths = (upright(sl[i : i + 1, :]).astype(jnp.int32) for i in range(1, 4))
    before = (owners == owner_row) & (iota((NDEV, NDEV), 1) < iota((NDEV, NDEV), 0))
    rank = jnp.sum(jnp.where(before, 1.0, 0.0), axis=1, keepdims=True)
    slot = rank * NDEV + owners
    twice = iota((NDEV, 128), 0) == lax.rem(iota((NDEV, 128), 1), NDEV)
    slot_row = jnp.sum(jnp.where(twice, slot, 0.0), axis=0, keepdims=True)
    routing = jnp.where(iota((128, 128), 0).astype(F32) == slot_row, 1.0, 0.0).astype(BF16)
    pick = jnp.where(lax.rem(iota((NDEV, 128), 1), NDEV) == columns, 1.0, 0.0).astype(BF16)
    lane = iota((NDEV, 128), 1)
    high = jnp.broadcast_to(offsets, (NDEV, 128)) >= 128
    inner = lax.rem(offsets, 128)
    spill = (lane < STRIP) & (inner > 128 - STRIP)
    bits = jnp.broadcast_to(inner, (NDEV, 128))
    zero8 = jnp.zeros((8, ROWS), F32)

    def fix_lon():
        to_east.wait_recv()
        to_west.wait_recv()
        for f in range(FIELDS):
            for l in range(LEVELS):
                out[f, l, 0:1] += d0 * hw[f, l]
                out[f, l, COLS - 1 : COLS] += d0 * he[f, l]

    def fix_lat(copy, buffer, tile, row):
        copy.wait_recv()
        halo = buffer[...]
        d = dif[1:2, tile : tile + 128]

        def fix(u, carry):
            f, l = lax.div(u, LEVELS), lax.rem(u, LEVELS)
            value = pltpu.roll(halo, lax.rem(128 + row - u, 128), 1)
            out[f, l, :, tile : tile + 128] += jnp.where(lane_u == row, d * value, 0.0)
            return carry

        lax.fori_loop(0, FIELDS * LEVELS, fix, 0, unroll=4)

    def fix_north():
        fix_lat(to_south, hn, 0, 0)

    def fix_south():
        fix_lat(to_north, hs, 128, 127)

    def strips_of(u, carry):
        x = out[lax.div(u, LEVELS), lax.rem(u, LEVELS)]
        top = x.astype(BF16).astype(F32)
        y = dot(pick, jnp.concatenate([top, zero8, x - top, zero8], 0).astype(BF16))
        a = jnp.where(high, y[:, 128:], y[:, :128])
        a = jnp.where(spill, y[:, 128:], a)
        for shift in (64, 32, 16):
            a = jnp.where((bits & shift) != 0, pltpu.roll(a, 128 - shift, 1), a)
        xs[u] = a
        return carry

    def cut_strips(first, last):
        lax.fori_loop(first, last, strips_of, 0, unroll=4)

    @pl.when(is_helper)
    def _():
        between = {
            7: fix_lon, 8: fix_north, 9: fix_south,
            11: lambda: cut_strips(0, 4), 12: lambda: cut_strips(4, 8), 13: lambda: cut_strips(8, 12)
        }
        for part in range(PARTS):
            pairs, s, r = pl.ds(part * SIZE, SIZE), s_fwd.at[part], r_fwd.at[part]
            for g in range(NZ):
                relay(part, g).wait_recv()

                def send(i, carry, g=g, pairs=pairs, s=s, r=r):
                    z = lax.rem(my_z + far_first(g), NZ)
                    d = z * NZ + (lax.rem(me, NZ) ^ (7 - i))
                    remote(rl.at[pairs, d], arr.at[pairs, me], s, r, la, d).start()
                    return carry

                lax.fori_loop(0, NZ - (g == NZ - 1), send, 0)
                if part * NZ + g in between:
                    between[part * NZ + g]()
            pltpu.make_async_copy(rl.at[pairs, me], arr.at[pairs, me], r).start()
        cut_strips(12, FIELDS * LEVELS)

    @pl.when(is_polar)
    def _():
        fix_lon()
        pl.when(has_north)(fix_north)
        pl.when(has_south)(fix_south)
        cut_strips(0, FIELDS * LEVELS)

    window = lax.div(lane, 32)
    for g in range(3):
        both = []
        for h in range(2):
            a = jnp.zeros((NDEV, 128), F32)
            for i in range(4):
                u = 8 * g + 2 * i + h
                if u < FIELDS * LEVELS:
                    v = xs[u] if i == 0 else pltpu.roll(xs[u], 32 * i, 1)
                    a = jnp.where(window == i, v, a)
            for shift in (8, 4, 2, 1):
                a = jnp.where((bits & shift) != 0, pltpu.roll(a, 128 - shift, 1), a)
            both.append(a)
        a = jnp.where(lax.rem(lane, 32) < 16, both[0], pltpu.roll(both[1], 16, 1))
        a = jnp.where(lax.rem(lane, STRIP) < lengths, a, 0.0)
        a = dot(routing, jnp.concatenate(split(a), 0))
        sb[g, 0] = a[:NDEV]
        sb[g, 1] = a[NDEV:]

    def send_nest():
        pltpu.make_async_copy(sb.at[:, :, me], rb.at[:, :, me], r_nest).start()

        def send(k, carry):
            d = peer(me, k)
            remote(sb.at[:, :, d], rb.at[:, :, me], s_nest, r_nest, la, d).start()
            return carry

        lax.fori_loop(0, NDEV - 1, send, 0)

    send_nest()

    cos, sin = tw[0], tw[1]
    lane_k, q = iota((QROWS, 128), 1), iota((QROWS, 128), 0)
    k1 = lax.rem(lane_k, 32)
    live = (q <= 32) & (k1 < K1)
    base = jnp.where(la < 2, 0, POLAR) + half * NDEV
    keep = live & (jnp.abs(q + 64 * (k1 - 14)) < cut[base + me])

    def filter_part(part):
        pairs, s, r = pl.ds(part * SIZE, SIZE), s_ret.at[part], r_ret.at[part]
        pltpu.make_async_copy(arr.at[pairs], arr.at[pairs], r_fwd.at[part]).wait()

        def forward(k, carry):
            hi, lo = split(arr[part * SIZE + k])
            y = dot(c1[...], jnp.concatenate([hi, lo, hi], 0))
            re, im = y[:QROWS], y[QROWS:]
            zb[k, :, 0:128] = re * cos + im * sin
            zb[k, :, 128:256] = im * cos - re * sin
            return carry

        lax.fori_loop(0, SIZE, forward, 0, unroll=True)
        hi, lo = split(zb[...].reshape(SIZE * QROWS, 256))
        spectrum = dot(jnp.concatenate([hi, lo, hi], 1), b1[...])
        spectrum = jnp.where(keep[None], spectrum.reshape(SIZE, QROWS, 128), 0.0)
        hi, lo = split(spectrum.reshape(SIZE * QROWS, 128))
        zb[...] = dot(jnp.concatenate([hi, lo, hi], 1), b2[...]).reshape(SIZE, QROWS, 256)

        def backward(k, carry):
            re, im = zb[k, :, 0:128], zb[k, :, 128:256]
            turned = jnp.concatenate([re * cos - im * sin, re * sin + im * cos], 0)
            hi, lo = split(turned)
            res[part * SIZE + k] = dot(c2[...], jnp.concatenate([hi, lo, hi], 0))
            return carry

        lax.fori_loop(0, SIZE, backward, 0, unroll=True)

        @pl.when(is_polar)
        def _():
            pltpu.make_async_copy(res.at[pairs, me], ret.at[pairs, 0, me], r).start()

        @pl.when(is_helper)
        def _():
            remote(res.at[pairs, me], ret.at[pairs, 1, me], s, r, polar_lat, me).start()

        def send_back(k, carry):
            d = peer(me, k)
            remote(res.at[pairs, d], ret.at[pairs, half, me], s, r, polar_lat, d).start()
            return carry

        lax.fori_loop(0, NDEV - 1, send_back, 0)

    for part in range(PARTS):
        filter_part(part)

    pltpu.make_async_copy(rb, rb, r_nest).wait()
    for g in range(3):
        tb[g] = jnp.concatenate([rb[g, 0], rb[g, 1]], 0).T
    for t in range(STRIP):
        x = jnp.concatenate([tb[g, pl.ds(t, 8, stride=STRIP), :] for g in range(3)], 0)
        top = x.astype(BF16).astype(F32)
        lb[:, t * 128 : (t + 1) * 128] = jnp.concatenate([top, x - top], 0).astype(BF16)
    places = npl[0].astype(F32)
    begin = jnp.concatenate([places[0:1], places[1:2]], 1)
    wide = 256
    point = iota((wide, 128), 0).astype(F32)

    def boundary(n, carry):
        first = pl.multiple_of(n * wide, wide)
        away = jnp.clip(point + (n * wide).astype(F32) - begin, -32.0, 224.0).astype(BF16)
        hats = []
        for t in range(STRIP):
            d = away - float(RATIO * t)
            hat = jnp.maximum(float(RATIO) - jnp.abs(d), 0.0)
            if t == 0:
                hat = jnp.where(d >= 0.0, hat, jnp.zeros_like(hat))
            hats.append(hat)
        total = lax.dot_general(
            lb[...], jnp.concatenate(hats, 1), (((1,), (1,)), ((), ())), preferred_element_type=F32
        )
        total = (total[:24] + total[24:]) * (1.0 / RATIO)
        for f in range(FIELDS):
            nest[0, f, :, pl.ds(first, wide)] = total[f * LEVELS : (f + 1) * LEVELS]
        return carry

    lax.fori_loop(0, NB // wide, boundary, 0, unroll=2)

    @pl.when(is_polar)
    def _():
        for part in range(PARTS):
            back = ret.at[pl.ds(part * SIZE, SIZE)]
            pltpu.make_async_copy(back, back, r_ret.at[part]).wait()

    to_east.wait_send()
    to_west.wait_send()
    pl.when(has_south)(to_south.wait_send)
    pl.when(has_north)(to_north.wait_send)
    others = pl.ds(0, NDEV - 1)
    pltpu.make_async_copy(sb.at[:, :, others], sb.at[:, :, others], s_nest).wait()
    for part in range(PARTS):
        gone = res.at[pl.ds(part * SIZE, SIZE), others]
        pltpu.make_async_copy(gone, gone, s_fwd.at[part]).wait()

    @pl.when(is_polar)
    def _():
        for part in range(PARTS):
            for g in range(NZ):
                relay(part, g).wait_send()
            gone = res.at[pl.ds(part * SIZE, SIZE), others]
            pltpu.make_async_copy(gone, gone, s_ret.at[part]).wait()

    @pl.when(is_helper)
    def _():
        for part in range(PARTS):
            gone = res.at[pl.ds(part * SIZE, SIZE)]
            pltpu.make_async_copy(gone, gone, s_ret.at[part]).wait()


def place_kernel(upd, nest, ret, out, nest_out, rows, sem):
    la = lax.axis_index("lat")
    is_polar = (la == 0) | (la == 3)
    start = pl.multiple_of(jnp.where(la == 3, ROWS - POLAR, 0), 128)
    other = pl.multiple_of(ROWS - POLAR - start, 128)
    nest_copy = pltpu.make_async_copy(nest, nest_out, sem.at[0])
    nest_copy.start()

    @pl.when(is_polar)
    def _():
        rest = (slice(None),) * 3 + (pl.ds(other, ROWS - POLAR),)
        rest_copy = pltpu.make_async_copy(upd.at[rest], out.at[rest], sem.at[1])
        rest_copy.start()
        copies = []
        for k in range(PAIRS):
            f, l0 = k // 2, 2 * (k % 2)
            turned = jnp.concatenate([ret[k, 0], ret[k, 1]], 0).T
            rows[f, l0] = turned[:COLS]
            rows[f, l0 + 1] = turned[64 : 64 + COLS]
            pair = pl.ds(l0, 2)
            copies.append(
                pltpu.make_async_copy(
                    rows.at[f, pair], out.at[f, pair, :, pl.ds(start, POLAR)], sem.at[2 + k]
                )
            )
            copies[k].start()
        rest_copy.wait()
        for copy in copies:
            copy.wait()

    @pl.when(jnp.logical_not(is_polar))
    def _():
        whole = pltpu.make_async_copy(upd, out, sem.at[1])
        whole.start()
        whole.wait()

    nest_copy.wait()


def local(model_state, diffusion, coupling, cutoff, strip_list, nest_place):
    vmem = pl.BlockSpec(memory_space=pltpu.VMEM)
    hbm = pl.BlockSpec(memory_space=pltpu.HBM)
    dma = pltpu.SemaphoreType.DMA
    args = [
        model_state,
        diffusion,
        jnp.transpose(coupling, (1, 0, 2)),
        cutoff,
        jnp.transpose(strip_list),
        jnp.transpose(nest_place, (0, 2, 1)),
        *[jnp.asarray(t) for t in tables()],
    ]
    spaces = [pltpu.SMEM if i in (2, 3) else pltpu.VMEM for i in range(len(args))]
    updated, nest, filtered = pl.pallas_call(
        step_kernel,
        name="dynamics_step",
        out_shape=[
            jax.ShapeDtypeStruct(model_state.shape, F32),
            jax.ShapeDtypeStruct((1, FIELDS, LEVELS, NB), F32),
            jax.ShapeDtypeStruct((PAIRS, 2, NDEV, 128), F32),
        ],
        in_specs=[hbm] * len(args),
        out_specs=[vmem, vmem, vmem],
        scratch_shapes=[
            *[space(a.shape, a.dtype) for space, a in zip(spaces, args)],
            dma((len(args),)),
            pltpu.VMEM((PAIRS, 2, NDEV, 128), F32),
            pltpu.VMEM((PAIRS, NDEV, 128), F32),
            pltpu.VMEM((PAIRS, NDEV, 128), F32),
            pltpu.VMEM((PAIRS, NDEV, 128), F32),
            pltpu.VMEM((SIZE, QROWS, 256), F32),
            pltpu.VMEM((COLS, 128), F32),
            pltpu.VMEM((COLS, 128), F32),
            pltpu.VMEM((FIELDS, LEVELS, 1, ROWS), F32),
            pltpu.VMEM((FIELDS, LEVELS, 1, ROWS), F32),
            pltpu.VMEM((COLS, 128), F32),
            pltpu.VMEM((COLS, 128), F32),
            pltpu.VMEM((FIELDS * LEVELS, NDEV, 128), F32),
            pltpu.VMEM((3, 2, NDEV, 128), F32),
            pltpu.VMEM((3, 2, NDEV, 128), F32),
            pltpu.VMEM((3, 128, 128), F32),
            pltpu.VMEM((48, STRIP * 128), BF16),
            dma((PARTS * NZ,)), dma((PARTS * NZ,)),
            dma((PARTS,)), dma((PARTS,)), dma((PARTS,)), dma((PARTS,)), dma, dma,
            dma((4,)), dma((4,)),
        ],
        compiler_params=pltpu.CompilerParams(
            collective_id=0, has_side_effects=True, vmem_limit_bytes=48 << 20
        ),
    )(*[pltpu.with_memory_space_constraint(a, pltpu.HBM) for a in args])
    return pl.pallas_call(
        place_kernel,
        name="place_filtered",
        out_shape=[
            jax.ShapeDtypeStruct(updated.shape, F32),
            jax.ShapeDtypeStruct(nest.shape, F32),
        ],
        in_specs=[vmem, vmem, vmem],
        out_specs=[hbm, hbm],
        scratch_shapes=[pltpu.VMEM((FIELDS, LEVELS, COLS, POLAR), F32), dma((2 + PAIRS,))],
        compiler_params=pltpu.CompilerParams(vmem_limit_bytes=16 << 20),
    )(updated, nest, filtered)


def solution(mesh):
    return jax.shard_map(
        local,
        mesh=mesh,
        in_specs=(
            P(None, None, "lon", "lat"),
            P(None, "lat"),
            P(),
            P(),
            P(("lat", "lon"), None),
            P(("lat", "lon"), None, None),
        ),
        out_specs=(P(None, None, "lon", "lat"), P(("lat", "lon"), None, None, None)),
        check_vma=False,
    )
```

```python
import jax
import jax.numpy as jnp
import ml_dtypes
import numpy as np
from jax import lax
from jax.experimental import pallas as pl
from jax.experimental.pallas import tpu as pltpu
from jax.sharding import PartitionSpec as P

MESH = pl.DeviceIdType.MESH
F32, BF16 = jnp.float32, jnp.bfloat16
FIELDS, LEVELS, COLS, ROWS = 5, 4, 56, 256
NLON, NDEV, POLAR, NB, RATIO, STRIP = 3584, 64, 128, 2048, 11, 16
PAIRS = FIELDS * LEVELS // 2
PARTS = 2
SIZE = PAIRS // PARTS
QROWS = 40
K1 = 28
NZ = 8


def hi_lo(table):
    hi = table.astype(np.float32).astype(ml_dtypes.bfloat16)
    lo = (table - hi.astype(np.float64)).astype(np.float32).astype(ml_dtypes.bfloat16)
    return hi, lo


def tables():
    q = np.arange(QROWS)
    live = (q <= 32).astype(np.float64)
    c = np.arange(NDEV)
    lane = np.arange(128)
    unit, mu = lane // 64, lane % 64
    m = np.where(mu == 57, -1, mu)
    live_in = (mu <= 57).astype(np.float64)
    live_out = (mu < COLS).astype(np.float64)
    turn = 2 * np.pi * np.outer(q, c) / NDEV
    c1 = np.concatenate([np.cos(turn) * live[:, None], -np.sin(turn) * live[:, None]], 0)
    weight = np.where((q == 0) | (q == 32), 1.0, 2.0) * live / NLON
    c2 = np.concatenate([np.cos(turn) * weight[:, None], -np.sin(turn) * weight[:, None]], 0).T
    phi = 2 * np.pi * np.outer(q, m) / NLON
    twiddle = np.stack([np.cos(phi), np.sin(phi)]) * live[None, :, None]
    out = np.arange(128)
    unit_k, part_k, j = out // 64, (out % 64) // 32, out % 32
    k1 = j - 14
    live_k = (j < K1).astype(np.float64)
    psi = 2 * np.pi * np.outer(m, k1) / COLS
    same = (unit[:, None] == unit_k[None, :]) * live_k[None, :]
    cos, sin = np.cos(psi) * same, np.sin(psi) * same
    real = part_k[None, :] == 0
    b1 = np.concatenate([np.where(real, cos, -sin), np.where(real, sin, cos)], 0)
    b1 = b1 * np.tile(live_in, 2)[:, None]
    b2 = np.concatenate([np.where(real, cos, -sin).T, np.where(real, sin, cos).T], 1)
    b2 = b2 * np.tile(live_out, 2)[None, :]
    def left(t):
        hi, lo = hi_lo(t)
        return np.concatenate([hi, hi, lo], 1)

    def right(t):
        hi, lo = hi_lo(t)
        return np.concatenate([hi, hi, lo], 0)

    return left(c1), twiddle.astype(np.float32), right(b1), right(b2), left(c2)


def split(x):
    hi = x.astype(BF16)
    return hi, (x - hi.astype(F32)).astype(BF16)


def iota(shape, dim):
    return lax.broadcasted_iota(jnp.int32, shape, dim)


def dot(a, b):
    return jnp.dot(a, b, preferred_element_type=F32)


def far_first(step):
    odd = lax.rem(step, 2) == 1
    return jnp.where(odd, 4 - lax.div(step + 1, 2), lax.rem(4 + lax.div(step, 2), NZ))


def peer(me, k):
    last = k >= 56
    side = jnp.where(k < 8, 0, lax.rem(k, 2))
    ring = jnp.where(k < 8, 0, 2 * lax.div(k - 8, 16) + 1 + side)
    inner = jnp.where(k < 8, k, lax.div(lax.rem(k - 8, 16), 2))
    ring = jnp.where(last, NZ - 1, ring)
    inner = 7 - jnp.where(last, k - 56, inner)
    z = lax.rem(lax.div(me, NZ) + far_first(ring), NZ)
    return z * NZ + (lax.rem(me, NZ) ^ inner)


def step_kernel(
    ms_hbm, dif_hbm, coup_hbm, cut_hbm, sl_hbm, npl_hbm, c1_hbm, tw_hbm, b1_hbm, b2_hbm, c2_hbm,
    out, nest, ret,
    ms, dif, coup, cut, sl, npl, c1, tw, b1, b2, c2, s_load,
    pk, rl, arr, res, zb, sn, ss, hw, he, hn, hs, xs, sb, rb, tb, lb,
    s_rel, r_rel, s_fwd, r_fwd, s_ret, r_ret, s_nest, r_nest, s_halo, r_halo,
):
    la, me = lax.axis_index("lat"), lax.axis_index("lon")
    polar_lat = jnp.where(la < 2, 0, 3)
    helper_lat = jnp.where(la < 2, 1, 2)
    is_polar = la == polar_lat
    is_helper = jnp.logical_not(is_polar)
    half = jnp.where(is_polar, 0, 1)
    start = pl.multiple_of(jnp.where(la == 3, ROWS - POLAR, 0), 128)
    has_north, has_south = la > 0, la < 3
    my_z = lax.div(me, NZ)

    def remote(src, dst, s, r, lat, lon):
        return pltpu.make_async_remote_copy(
            src, dst, s, r, device_id={"lat": lat, "lon": lon}, device_id_type=MESH
        )

    early = [(ms_hbm, ms), (dif_hbm, dif), (coup_hbm, coup)]
    late = [(cut_hbm, cut), (sl_hbm, sl), (npl_hbm, npl), (c1_hbm, c1), (tw_hbm, tw)]
    late += [(b1_hbm, b1), (b2_hbm, b2), (c2_hbm, c2)]
    loads = [pltpu.make_async_copy(a, b, s_load.at[i]) for i, (a, b) in enumerate(early + late)]
    for load in loads:
        load.start()

    barrier = pltpu.get_barrier_semaphore()

    def greet(lat, lon):
        pl.semaphore_signal(barrier, device_id={"lat": lat, "lon": lon}, device_id_type=MESH)

    @pl.when(has_north)
    def _():
        greet(la - 1, me)

    @pl.when(has_south)
    def _():
        greet(la + 1, me)

    def greet_plane(k, carry):
        greet(la, peer(me, k))
        return carry

    lax.fori_loop(0, NDEV - 1, greet_plane, 0)
    for load in loads[: len(early)]:
        load.wait()

    d0, d1 = dif[0:1, :], dif[1:2, :]
    lane_row = iota((COLS, ROWS), 1)
    col = iota((COLS, ROWS), 0)
    lane_u = iota((COLS, 128), 1)
    sn[...] = jnp.zeros_like(sn)
    ss[...] = jnp.zeros_like(ss)

    def level(l, carry):
        x = [ms[g, l] for g in range(FIELDS)]
        for f in range(FIELDS):
            own = x[f]
            east = jnp.where(col == COLS - 1, 0.0, pltpu.roll(own, COLS - 1, 0))
            west = jnp.where(col == 0, 0.0, pltpu.roll(own, 1, 0))
            south = jnp.where(lane_row == ROWS - 1, 0.0, pltpu.roll(own, ROWS - 1, 1))
            north = jnp.where(lane_row == 0, 0.0, pltpu.roll(own, 1, 1))
            acc = own + d0 * (east + west - 2.0 * own) + d1 * (north + south - 2.0 * own)
            for g in range(FIELDS):
                acc = acc + coup[f, l, g] * x[g]
            out[f, l] = acc
            u = f * LEVELS + l
            sn[...] = jnp.where(lane_u == u, own[:, 0:1], sn[...])
            ss[...] = jnp.where(lane_u == u, own[:, ROWS - 1 : ROWS], ss[...])
        return carry

    lax.fori_loop(0, LEVELS, level, 0, unroll=2)

    @pl.when(is_polar)
    def _():
        tail_row = iota((8, 128), 0)
        d0p = dif[0:1, pl.ds(start, POLAR)]

        def pack(k, carry):
            f, l0 = lax.div(k, 2), 2 * lax.rem(k, 2)
            rows = []
            for p in range(2):
                first = ms[f, l0 + p, 0:1, pl.ds(start, POLAR)]
                last = ms[f, l0 + p, COLS - 1 : COLS, pl.ds(start, POLAR)]
                tail = jnp.where(tail_row == 0, last, jnp.where(tail_row == 1, first, 0.0)) * d0p
                rows += [out[f, l0 + p, :, pl.ds(start, POLAR)], tail]
            turned = jnp.concatenate(rows, 0).T
            pk[k, 0] = turned[:NDEV]
            pk[k, 1] = turned[NDEV:]
            return carry

        lax.fori_loop(0, PAIRS, pack, 0, unroll=5)

    pl.semaphore_wait(barrier, NDEV - 1 + jnp.where(is_polar, 1, 2))

    east_dev, west_dev = lax.rem(me + 1, NDEV), lax.rem(me + NDEV - 1, NDEV)
    to_east = remote(ms.at[:, :, pl.ds(COLS - 1, 1)], hw, s_halo.at[0], r_halo.at[0], la, east_dev)
    to_west = remote(ms.at[:, :, pl.ds(0, 1)], he, s_halo.at[1], r_halo.at[1], la, west_dev)
    to_south = remote(ss, hn, s_halo.at[2], r_halo.at[2], jnp.minimum(la + 1, 3), me)
    to_north = remote(sn, hs, s_halo.at[3], r_halo.at[3], jnp.maximum(la - 1, 0), me)


    def relay(part, g):
        rows = pl.ds(lax.rem(my_z + far_first(g), NZ) * NZ, NZ)
        pairs, i = pl.ds(part * SIZE, SIZE), part * NZ + g
        return remote(
            pk.at[pairs, 1, rows], rl.at[pairs, rows], s_rel.at[i], r_rel.at[i], helper_lat, me
        )

    to_east.start()
    to_west.start()
    pl.when(has_south)(to_south.start)
    pl.when(has_north)(to_north.start)

    @pl.when(is_polar)
    def _():
        for part in range(PARTS):
            for g in range(NZ):
                relay(part, g).start()

    @pl.when(is_polar)
    def _():
        for part in range(PARTS):
            pairs, s, r = pl.ds(part * SIZE, SIZE), s_fwd.at[part], r_fwd.at[part]
            pltpu.make_async_copy(pk.at[pairs, 0, me], arr.at[pairs, me], r).start()

            def send(k, carry, pairs=pairs, s=s, r=r):
                d = peer(me, k)
                remote(pk.at[pairs, 0, d], arr.at[pairs, me], s, r, la, d).start()
                return carry

            lax.fori_loop(0, NDEV - 1, send, 0)

    for load in loads[len(early) :]:
        load.wait()

    eye = iota((NDEV, NDEV), 0) == iota((NDEV, NDEV), 1)

    def upright(row):
        return jnp.sum(jnp.where(eye, row.astype(F32), 0.0), axis=1, keepdims=True)

    owner_row = sl[0:1, :].astype(F32)
    owners = upright(owner_row)
    columns, offsets, lengths = (upright(sl[i : i + 1, :]).astype(jnp.int32) for i in range(1, 4))
    before = (owners == owner_row) & (iota((NDEV, NDEV), 1) < iota((NDEV, NDEV), 0))
    rank = jnp.sum(jnp.where(before, 1.0, 0.0), axis=1, keepdims=True)
    slot = rank * NDEV + owners
    twice = iota((NDEV, 128), 0) == lax.rem(iota((NDEV, 128), 1), NDEV)
    slot_row = jnp.sum(jnp.where(twice, slot, 0.0), axis=0, keepdims=True)
    routing = jnp.where(iota((128, 128), 0).astype(F32) == slot_row, 1.0, 0.0).astype(BF16)
    pick = jnp.where(lax.rem(iota((NDEV, 128), 1), NDEV) == columns, 1.0, 0.0).astype(BF16)
    lane = iota((NDEV, 128), 1)
    high = jnp.broadcast_to(offsets, (NDEV, 128)) >= 128
    inner = lax.rem(offsets, 128)
    spill = (lane < STRIP) & (inner > 128 - STRIP)
    bits = jnp.broadcast_to(inner, (NDEV, 128))
    zero8 = jnp.zeros((8, ROWS), F32)

    def fix_lon():
        to_east.wait_recv()
        to_west.wait_recv()
        for f in range(FIELDS):
            for l in range(LEVELS):
                out[f, l, 0:1] += d0 * hw[f, l]
                out[f, l, COLS - 1 : COLS] += d0 * he[f, l]

    def fix_lat(copy, buffer, tile, row):
        copy.wait_recv()
        halo = buffer[...]
        d = dif[1:2, tile : tile + 128]

        def fix(u, carry):
            f, l = lax.div(u, LEVELS), lax.rem(u, LEVELS)
            value = pltpu.roll(halo, lax.rem(128 + row - u, 128), 1)
            out[f, l, :, tile : tile + 128] += jnp.where(lane_u == row, d * value, 0.0)
            return carry

        lax.fori_loop(0, FIELDS * LEVELS, fix, 0, unroll=4)

    def fix_north():
        fix_lat(to_south, hn, 0, 0)

    def fix_south():
        fix_lat(to_north, hs, 128, 127)

    def strips_of(u, carry):
        x = out[lax.div(u, LEVELS), lax.rem(u, LEVELS)]
        top = x.astype(BF16).astype(F32)
        y = dot(pick, jnp.concatenate([top, zero8, x - top, zero8], 0).astype(BF16))
        a = jnp.where(high, y[:, 128:], y[:, :128])
        a = jnp.where(spill, y[:, 128:], a)
        for shift in (64, 32, 16):
            a = jnp.where((bits & shift) != 0, pltpu.roll(a, 128 - shift, 1), a)
        xs[u] = a
        return carry

    def cut_strips(first, last):
        lax.fori_loop(first, last, strips_of, 0, unroll=4)

    @pl.when(is_helper)
    def _():
        between = {
            7: fix_lon, 8: fix_north, 9: fix_south,
            11: lambda: cut_strips(0, 4), 12: lambda: cut_strips(4, 8), 13: lambda: cut_strips(8, 12)
        }
        for part in range(PARTS):
            pairs, s, r = pl.ds(part * SIZE, SIZE), s_fwd.at[part], r_fwd.at[part]
            for g in range(NZ):
                relay(part, g).wait_recv()

                def send(i, carry, g=g, pairs=pairs, s=s, r=r):
                    z = lax.rem(my_z + far_first(g), NZ)
                    d = z * NZ + (lax.rem(me, NZ) ^ (7 - i))
                    remote(rl.at[pairs, d], arr.at[pairs, me], s, r, la, d).start()
                    return carry

                lax.fori_loop(0, NZ - (g == NZ - 1), send, 0)
                if part * NZ + g in between:
                    between[part * NZ + g]()
            pltpu.make_async_copy(rl.at[pairs, me], arr.at[pairs, me], r).start()
        cut_strips(12, FIELDS * LEVELS)

    @pl.when(is_polar)
    def _():
        fix_lon()
        pl.when(has_north)(fix_north)
        pl.when(has_south)(fix_south)
        cut_strips(0, FIELDS * LEVELS)

    window = lax.div(lane, 32)
    for g in range(3):
        both = []
        for h in range(2):
            a = jnp.zeros((NDEV, 128), F32)
            for i in range(4):
                u = 8 * g + 2 * i + h
                if u < FIELDS * LEVELS:
                    v = xs[u] if i == 0 else pltpu.roll(xs[u], 32 * i, 1)
                    a = jnp.where(window == i, v, a)
            for shift in (8, 4, 2, 1):
                a = jnp.where((bits & shift) != 0, pltpu.roll(a, 128 - shift, 1), a)
            both.append(a)
        a = jnp.where(lax.rem(lane, 32) < 16, both[0], pltpu.roll(both[1], 16, 1))
        a = jnp.where(lax.rem(lane, STRIP) < lengths, a, 0.0)
        a = dot(routing, jnp.concatenate(split(a), 0))
        sb[g, 0] = a[:NDEV]
        sb[g, 1] = a[NDEV:]

    def send_nest():
        pltpu.make_async_copy(sb.at[:, :, me], rb.at[:, :, me], r_nest).start()

        def send(k, carry):
            d = peer(me, k)
            remote(sb.at[:, :, d], rb.at[:, :, me], s_nest, r_nest, la, d).start()
            return carry

        lax.fori_loop(0, NDEV - 1, send, 0)

    send_nest()

    cos, sin = tw[0], tw[1]
    lane_k, q = iota((QROWS, 128), 1), iota((QROWS, 128), 0)
    k1 = lax.rem(lane_k, 32)
    live = (q <= 32) & (k1 < K1)
    base = jnp.where(la < 2, 0, POLAR) + half * NDEV
    keep = live & (jnp.abs(q + 64 * (k1 - 14)) < cut[base + me])

    def filter_part(part):
        pairs, s, r = pl.ds(part * SIZE, SIZE), s_ret.at[part], r_ret.at[part]
        pltpu.make_async_copy(arr.at[pairs], arr.at[pairs], r_fwd.at[part]).wait()

        def forward(k, carry):
            hi, lo = split(arr[part * SIZE + k])
            y = dot(c1[...], jnp.concatenate([hi, lo, hi], 0))
            re, im = y[:QROWS], y[QROWS:]
            zb[k, :, 0:128] = re * cos + im * sin
            zb[k, :, 128:256] = im * cos - re * sin
            return carry

        lax.fori_loop(0, SIZE, forward, 0, unroll=True)
        hi, lo = split(zb[...].reshape(SIZE * QROWS, 256))
        spectrum = dot(jnp.concatenate([hi, lo, hi], 1), b1[...])
        spectrum = jnp.where(keep[None], spectrum.reshape(SIZE, QROWS, 128), 0.0)
        hi, lo = split(spectrum.reshape(SIZE * QROWS, 128))
        zb[...] = dot(jnp.concatenate([hi, lo, hi], 1), b2[...]).reshape(SIZE, QROWS, 256)

        def backward(k, carry):
            re, im = zb[k, :, 0:128], zb[k, :, 128:256]
            turned = jnp.concatenate([re * cos - im * sin, re * sin + im * cos], 0)
            hi, lo = split(turned)
            res[part * SIZE + k] = dot(c2[...], jnp.concatenate([hi, lo, hi], 0))
            return carry

        lax.fori_loop(0, SIZE, backward, 0, unroll=True)

        @pl.when(is_polar)
        def _():
            pltpu.make_async_copy(res.at[pairs, me], ret.at[pairs, 0, me], r).start()

        @pl.when(is_helper)
        def _():
            remote(res.at[pairs, me], ret.at[pairs, 1, me], s, r, polar_lat, me).start()

        def send_back(k, carry):
            d = peer(me, k)
            remote(res.at[pairs, d], ret.at[pairs, half, me], s, r, polar_lat, d).start()
            return carry

        lax.fori_loop(0, NDEV - 1, send_back, 0)

    for part in range(PARTS):
        filter_part(part)

    pltpu.make_async_copy(rb, rb, r_nest).wait()
    for g in range(3):
        tb[g] = jnp.concatenate([rb[g, 0], rb[g, 1]], 0).T
    for t in range(STRIP):
        x = jnp.concatenate([tb[g, pl.ds(t, 8, stride=STRIP), :] for g in range(3)], 0)
        top = x.astype(BF16).astype(F32)
        lb[:, t * 128 : (t + 1) * 128] = jnp.concatenate([top, x - top], 0).astype(BF16)
    places = npl[0].astype(F32)
    begin = jnp.concatenate([places[0:1], places[1:2]], 1)
    wide = 256
    point = iota((wide, 128), 0).astype(F32)

    def boundary(n, carry):
        first = pl.multiple_of(n * wide, wide)
        away = jnp.clip(point + (n * wide).astype(F32) - begin, -32.0, 224.0).astype(BF16)
        hats = []
        for t in range(STRIP):
            d = away - float(RATIO * t)
            hat = jnp.maximum(float(RATIO) - jnp.abs(d), 0.0)
            if t == 0:
                hat = jnp.where(d >= 0.0, hat, jnp.zeros_like(hat))
            hats.append(hat)
        total = lax.dot_general(
            lb[...], jnp.concatenate(hats, 1), (((1,), (1,)), ((), ())), preferred_element_type=F32
        )
        total = (total[:24] + total[24:]) * (1.0 / RATIO)
        for f in range(FIELDS):
            nest[0, f, :, pl.ds(first, wide)] = total[f * LEVELS : (f + 1) * LEVELS]
        return carry

    lax.fori_loop(0, NB // wide, boundary, 0, unroll=2)

    @pl.when(is_polar)
    def _():
        for part in range(PARTS):
            back = ret.at[pl.ds(part * SIZE, SIZE)]
            pltpu.make_async_copy(back, back, r_ret.at[part]).wait()

    to_east.wait_send()
    to_west.wait_send()
    pl.when(has_south)(to_south.wait_send)
    pl.when(has_north)(to_north.wait_send)
    others = pl.ds(0, NDEV - 1)
    pltpu.make_async_copy(sb.at[:, :, others], sb.at[:, :, others], s_nest).wait()
    for part in range(PARTS):
        gone = res.at[pl.ds(part * SIZE, SIZE), others]
        pltpu.make_async_copy(gone, gone, s_fwd.at[part]).wait()

    @pl.when(is_polar)
    def _():
        for part in range(PARTS):
            for g in range(NZ):
                relay(part, g).wait_send()
            gone = res.at[pl.ds(part * SIZE, SIZE), others]
            pltpu.make_async_copy(gone, gone, s_ret.at[part]).wait()

    @pl.when(is_helper)
    def _():
        for part in range(PARTS):
            gone = res.at[pl.ds(part * SIZE, SIZE)]
            pltpu.make_async_copy(gone, gone, s_ret.at[part]).wait()


def place_kernel(upd, nest, ret, out, nest_out, rows, sem):
    la = lax.axis_index("lat")
    is_polar = (la == 0) | (la == 3)
    start = pl.multiple_of(jnp.where(la == 3, ROWS - POLAR, 0), 128)
    other = pl.multiple_of(ROWS - POLAR - start, 128)
    nest_copy = pltpu.make_async_copy(nest, nest_out, sem.at[0])
    nest_copy.start()

    @pl.when(is_polar)
    def _():
        rest = (slice(None),) * 3 + (pl.ds(other, ROWS - POLAR),)
        rest_copy = pltpu.make_async_copy(upd.at[rest], out.at[rest], sem.at[1])
        rest_copy.start()
        copies = []
        for k in range(PAIRS):
            f, l0 = k // 2, 2 * (k % 2)
            turned = jnp.concatenate([ret[k, 0], ret[k, 1]], 0).T
            rows[f, l0] = turned[:COLS]
            rows[f, l0 + 1] = turned[64 : 64 + COLS]
            pair = pl.ds(l0, 2)
            copies.append(
                pltpu.make_async_copy(
                    rows.at[f, pair], out.at[f, pair, :, pl.ds(start, POLAR)], sem.at[2 + k]
                )
            )
            copies[k].start()
        rest_copy.wait()
        for copy in copies:
            copy.wait()

    @pl.when(jnp.logical_not(is_polar))
    def _():
        whole = pltpu.make_async_copy(upd, out, sem.at[1])
        whole.start()
        whole.wait()

    nest_copy.wait()


def local(model_state, diffusion, coupling, cutoff, strip_list, nest_place):
    vmem = pl.BlockSpec(memory_space=pltpu.VMEM)
    hbm = pl.BlockSpec(memory_space=pltpu.HBM)
    dma = pltpu.SemaphoreType.DMA
    args = [
        model_state,
        diffusion,
        jnp.transpose(coupling, (1, 0, 2)),
        cutoff,
        jnp.transpose(strip_list),
        jnp.transpose(nest_place, (0, 2, 1)),
        *[jnp.asarray(t) for t in tables()],
    ]
    spaces = [pltpu.SMEM if i in (2, 3) else pltpu.VMEM for i in range(len(args))]
    updated, nest, filtered = pl.pallas_call(
        step_kernel,
        name="dynamics_step",
        out_shape=[
            jax.ShapeDtypeStruct(model_state.shape, F32),
            jax.ShapeDtypeStruct((1, FIELDS, LEVELS, NB), F32),
            jax.ShapeDtypeStruct((PAIRS, 2, NDEV, 128), F32),
        ],
        in_specs=[hbm] * len(args),
        out_specs=[vmem, vmem, vmem],
        scratch_shapes=[
            *[space(a.shape, a.dtype) for space, a in zip(spaces, args)],
            dma((len(args),)),
            pltpu.VMEM((PAIRS, 2, NDEV, 128), F32),
            pltpu.VMEM((PAIRS, NDEV, 128), F32),
            pltpu.VMEM((PAIRS, NDEV, 128), F32),
            pltpu.VMEM((PAIRS, NDEV, 128), F32),
            pltpu.VMEM((SIZE, QROWS, 256), F32),
            pltpu.VMEM((COLS, 128), F32),
            pltpu.VMEM((COLS, 128), F32),
            pltpu.VMEM((FIELDS, LEVELS, 1, ROWS), F32),
            pltpu.VMEM((FIELDS, LEVELS, 1, ROWS), F32),
            pltpu.VMEM((COLS, 128), F32),
            pltpu.VMEM((COLS, 128), F32),
            pltpu.VMEM((FIELDS * LEVELS, NDEV, 128), F32),
            pltpu.VMEM((3, 2, NDEV, 128), F32),
            pltpu.VMEM((3, 2, NDEV, 128), F32),
            pltpu.VMEM((3, 128, 128), F32),
            pltpu.VMEM((48, STRIP * 128), BF16),
            dma((PARTS * NZ,)), dma((PARTS * NZ,)),
            dma((PARTS,)), dma((PARTS,)), dma((PARTS,)), dma((PARTS,)), dma, dma,
            dma((4,)), dma((4,)),
        ],
        compiler_params=pltpu.CompilerParams(
            collective_id=0, has_side_effects=True, vmem_limit_bytes=48 << 20
        ),
    )(*[pltpu.with_memory_space_constraint(a, pltpu.HBM) for a in args])
    return pl.pallas_call(
        place_kernel,
        name="place_filtered",
        out_shape=[
            jax.ShapeDtypeStruct(updated.shape, F32),
            jax.ShapeDtypeStruct(nest.shape, F32),
        ],
        in_specs=[vmem, vmem, vmem],
        out_specs=[hbm, hbm],
        scratch_shapes=[pltpu.VMEM((FIELDS, LEVELS, COLS, POLAR), F32), dma((2 + PAIRS,))],
        compiler_params=pltpu.CompilerParams(vmem_limit_bytes=16 << 20),
    )(updated, nest, filtered)


def solution(mesh):
    return jax.shard_map(
        local,
        mesh=mesh,
        in_specs=(
            P(None, None, "lon", "lat"),
            P(None, "lat"),
            P(),
            P(),
            P(("lat", "lon"), None),
            P(("lat", "lon"), None, None),
        ),
        out_specs=(P(None, None, "lon", "lat"), P(("lat", "lon"), None, None, None)),
        check_vma=False,
    )
```
